128 devices in a mesh: dp: 8 (over z, core), clus: 16 (over y, x).
Axes of the slice: x: 4, y: 4, z: 4, core: 2. Of those that a mesh axis runs over, the one named last changes fastest.
Arguments:
- points: bfloat16 [512, 128, 1024], P(('dp', 'clus')), may hold values from -40 to 40
- block_cluster: int32 [512, 1], P(('dp', 'clus')), may hold values from 0 to 255, as said below
- queries: bfloat16 [2048, 1024], P(('dp', 'clus')), may hold values from -6 to 6
- query_ids: int32 [256, 128], P(('dp', 'clus')), may hold values from 0 to 2047
Outputs:
- gram_tiles: float32 [256, 1024, 1024], P(('dp', 'clus'))
- cross: float32 [256, 1024, 128], P(('dp', 'clus'))
The draws below stay inside these ranges and needn't reach their ends.
Inputs may be any that keep to these rules, and one draw needn't show every extreme that they name: `block_cluster`: cluster c is owned by the device at position c // 2 in the order of dp+clus, dp slowest. Of the 4 blocks of one device, at most 2 belong to clusters whose owners share one index along clus, exactly 2 for some device and index. Of all blocks on the devices of one index along dp, those whose owners share one index along clus number at most 3 for each owner index along dp, exactly 3 for some.
All inputs are finite; a program needn't handle non-finite values.
Results may differ from the reference program's by a relative error of at most 0.0022.
Values may be sent and summed in bfloat16 or wider, within the bound.
A program may use at most 128 MiB of HBM per device.

```python
import math
import jax
import jax.numpy as jnp
from jax import lax

D = 1024
BLK = 128
CL_OWN = 2
MQ = 128
CLUSTERS = 256
NB = 4
BLOCKS = 512
NQ = 2048
MEANROWS = 256
CB = 3
N_DP = 8
N_CLUS = 16


def draw_points(key, part):
    keys = jax.random.split(jax.random.fold_in(key, 5), 3)
    row_scale = jnp.exp(jax.random.uniform(keys[0], (BLOCKS, BLK, 1), jnp.float32, math.log(0.25), math.log(2.5)))
    col_scale = jnp.exp(jax.random.uniform(keys[1], (1, 1, D), jnp.float32, math.log(0.4), math.log(4.0)))
    base = jnp.clip(jax.random.normal(keys[2], (BLOCKS, BLK, D), jnp.float32), -4.0, 4.0)
    return (base * row_scale * col_scale).astype(jnp.bfloat16)


def draw_row_routes(row_key):
    full_cap = N_DP * CB
    others = N_CLUS - 1
    keys = jax.random.split(row_key, 7)
    col_order = jax.random.permutation(keys[0], N_CLUS).astype(jnp.int32)
    slot_count = others * full_cap
    slot_index = jnp.arange(slot_count, dtype=jnp.int32)
    slot_col = slot_index // full_cap
    col_weight = jax.random.randint(keys[1], (others,), 1, 5).astype(jnp.int32)
    noise = jax.random.randint(keys[2], (slot_count,), 0, 1024).astype(jnp.int32)
    priority = noise * col_weight[slot_col] * slot_count + slot_index
    chosen_order = jnp.argsort(priority, stable=True)
    remaining = N_CLUS * NB - full_cap
    chosen = jnp.zeros((slot_count,), jnp.int32).at[chosen_order[:remaining]].set(1)
    counts_other = jnp.sum(chosen.reshape(others, full_cap), axis=1)
    counts = jnp.concatenate([jnp.full((1,), full_cap, jnp.int32), counts_other.astype(jnp.int32)])
    ends = jnp.cumsum(counts).astype(jnp.int32)
    starts = ends - counts
    token = jnp.arange(N_CLUS * NB, dtype=jnp.int32)
    token_col = jnp.sum((token[:, None] >= ends[None, :]).astype(jnp.int32), axis=1)
    rank_in_col = token - starts[token_col]
    perm_keys = jax.random.split(keys[3], N_CLUS)
    perms = jax.vmap(lambda one_key: jax.random.permutation(one_key, full_cap))(perm_keys).astype(jnp.int32)
    target_dp = perms[token_col, rank_in_col] // CB
    local = jax.random.randint(keys[4], (N_CLUS * NB,), 0, CL_OWN).astype(jnp.int32)
    cluster = (target_dp * N_CLUS + col_order[token_col]) * CL_OWN + local
    by_position = cluster.reshape(NB, N_CLUS).T
    shuffle_keys = jax.random.split(keys[5], N_CLUS)
    orders = jax.vmap(lambda one_key: jax.random.permutation(one_key, NB))(shuffle_keys).astype(jnp.int32)
    by_position = jnp.take_along_axis(by_position, orders, axis=1)
    source_perm = jax.random.permutation(keys[6], N_CLUS).astype(jnp.int32)
    inverse = jnp.argsort(source_perm, stable=True)
    return by_position[inverse]


def draw_block_cluster(key, part):
    row_keys = jax.random.split(jax.random.fold_in(key, 11), N_DP)
    table = jax.vmap(draw_row_routes)(row_keys)
    return table.reshape(BLOCKS, 1).astype(jnp.int32)


def touch_ends(values, key, smallest, top_value):
    place = [jax.random.randint(jax.random.fold_in(key, axis), (), 0, length) for axis, length in enumerate(values.shape)]
    widest = values.shape.index(max(values.shape))
    neighbour = place[:widest] + [(place[widest] + 1) % values.shape[widest]] + place[widest + 1:]
    return values.at[tuple(place)].set(smallest).at[tuple(neighbour)].set(top_value)


def block_levels(key, shape, shards, low, top_value):
    factor_of, own = 1.0, jax.random.fold_in(key, 6)
    for dim, blocks in shards:
        steps = jnp.exp(jax.random.uniform(jax.random.fold_in(own, dim), (blocks,), jnp.float32, low / len(shards), top_value / len(shards)))
        factor_of = factor_of * jnp.repeat(steps, shape[dim] // blocks).reshape([-1 if axis == dim else 1 for axis in range(len(shape))])
    return factor_of


def normal_values(stream_key, dims, scale, bound, shards=(), kind=jnp.bfloat16):
    values = scale * jax.random.normal(stream_key, dims, jnp.float32)
    if shards:
        values = values * block_levels(stream_key, dims, shards, -0.22, 0.18)
    return jnp.clip(values, -bound, bound).astype(kind)


def setup_inputs(seed: int = 0) -> dict:
    splits = jax.random.split(jax.random.key(seed), 5)
    return {
        "points": draw_points(jax.random.fold_in(splits[4], 71), 0),
        "block_cluster": draw_block_cluster(jax.random.fold_in(splits[4], 71), 0),
        "queries": normal_values(splits[2], (NQ, D), 1.0, 6.0, ((0, 128),)),
        "query_ids": touch_ends(jax.random.randint(splits[3], (CLUSTERS, MQ), 0, NQ), jax.random.fold_in(splits[3], 1), 0, NQ - 1).astype(jnp.int32),
    }


def reference(points, block_cluster, queries, query_ids):

    def add_block(index, carry):
        gram_acc, cross_acc = carry
        which = block_cluster[index, 0].astype(jnp.int32)
        block = lax.dynamic_index_in_dim(points, index, 0, keepdims=False)
        wanted = lax.dynamic_index_in_dim(query_ids, which, 0, keepdims=False).astype(jnp.int32)
        train_rows = queries[wanted]
        row_weight = lax.rsqrt(lax.optimization_barrier(jnp.mean(jnp.square(block.astype(jnp.float32)), axis=1)) + 1e-06)
        raw = jnp.dot(train_rows, block.T, preferred_element_type=jnp.float32)
        scores = (raw * row_weight[None, :]).astype(jnp.bfloat16)
        gram_acc = gram_acc.at[which].add(jnp.dot(block.T, block, preferred_element_type=jnp.float32))
        cross_acc = cross_acc.at[which].add(jnp.dot(block.T, scores.T, preferred_element_type=jnp.float32))
        return (gram_acc, cross_acc)
    gram_init = jnp.zeros((CLUSTERS, D, D), jnp.float32)
    cross_init = jnp.zeros((CLUSTERS, D, MQ), jnp.float32)
    gram_acc, cross_acc = lax.fori_loop(0, BLOCKS, add_block, (gram_init, cross_init))
    factor = 1.0 / MEANROWS
    return (gram_acc * factor, cross_acc * factor)
```

```python
import functools

import jax
import jax.numpy as jnp
from jax import lax
from jax.experimental import pallas as pl
from jax.experimental.pallas import tpu as pltpu
from jax.sharding import PartitionSpec as P

MEANROWS = 256
MESH = pl.DeviceIdType.MESH
RING = 4
MID_CAP = 8
OWN_CAP = 3
ROWS = 16
COL_SPLIT = 2


def one_hot_pick(values, mask, rank, count):
    slot = lax.broadcasted_iota(jnp.int32, (count,) + mask.shape, 0)
    hit = mask[None] & (rank[None] == slot)
    return jnp.sum(jnp.where(hit, values, 0), axis=-1)


def before(mask):
    n = mask.shape[-1]
    row = lax.broadcasted_iota(jnp.int32, (n, n), 0)
    col = lax.broadcasted_iota(jnp.int32, (n, n), 1)
    return jnp.sum((mask[..., None, :] & (col < row)).astype(jnp.int32), axis=-1)


def tables(labels, dp, cl, cl_own, n_dp, n_clus, nb):
    y, x = cl // RING, cl % RING
    per_row = n_clus * nb
    row = lax.dynamic_index_in_dim(labels, dp, 0, keepdims=False)
    col = row // cl_own % n_clus
    dest = row // cl_own // n_clus
    grid = col.reshape(RING, RING, nb)
    pos = jnp.arange(RING, dtype=jnp.int32)
    local = jnp.arange(RING * nb, dtype=jnp.int32)
    ring_x = lax.dynamic_index_in_dim(grid, y, 0, keepdims=False).reshape(RING * nb)
    ring_y = lax.dynamic_index_in_dim(grid, x, 1, keepdims=False).reshape(RING * nb)
    mask_a = ring_x[None, :] == (pos * RING + x)[:, None]
    mask_b = ring_y[None, :] == (y * RING + pos)[:, None]
    pick_a = one_hot_pick(local, mask_a, before(mask_a), MID_CAP).T
    pick_b = one_hot_pick(local, mask_b, before(mask_b), MID_CAP).T
    mine = grid == cl
    mine_a = mine.reshape(RING, RING * nb)
    mine_b = mine.transpose(1, 0, 2).reshape(RING, RING * nb)
    at_a = (before(mine_a) + pos[:, None] * MID_CAP).reshape(per_row)
    at_b = (before(mine_b) + pos[:, None] * MID_CAP).reshape(RING, RING, nb).transpose(1, 0, 2).reshape(per_row)
    to_row = mine.reshape(1, per_row) & (dest[None, :] == jnp.arange(n_dp, dtype=jnp.int32)[:, None])
    rank = before(to_row)
    send_a = one_hot_pick(at_a, to_row, rank, OWN_CAP).T
    send_b = one_hot_pick(at_b, to_row, rank, OWN_CAP).T
    route = jnp.concatenate([t.reshape(-1) for t in (pick_a, pick_b, send_a, send_b)]).astype(jnp.int32)
    here = dp * n_clus + cl
    owned = labels // cl_own == here
    rank_all = before(owned)
    slot_local = one_hot_pick(labels % cl_own + 1, owned, rank_all, OWN_CAP).T.reshape(-1) - 1
    return route, slot_local


def place_slots(slot_local, cl_own):
    position = jnp.full(slot_local.shape, -1, jnp.int32)
    base = jnp.zeros((), jnp.int32)
    counts, bases = [], []
    for owned in range(cl_own):
        mask = slot_local == owned
        count = jnp.sum(mask.astype(jnp.int32))
        position = jnp.where(mask, base + before(mask), position)
        counts.append(count)
        bases.append(base)
        base = base + (count + 1) // 2 * 2
    return jnp.concatenate([position, jnp.stack(counts + bases)]).astype(jnp.int32)


def route_kernel(nb, blk, width, n_dp, tab, pts, out, *scratch):
    pieces = []
    half = blk // 2
    wide = width // COL_SPLIT
    for row0 in range(0, half, ROWS):
        for c0 in range(0, width, wide):
            pieces.append((row0, c0))
    steps = len(pieces)
    total = 2 * steps
    got1, pack2, got2, pack3 = (scratch[i * total:(i + 1) * total] for i in range(4))
    s1, r1, s2, r2, s3, r3, own = scratch[4 * total:]
    dp = lax.axis_index("dp")
    cl = lax.axis_index("clus")
    y, x = lax.div(cl, RING), lax.rem(cl, RING)

    def peer(cls, stage, delta):
        along_x = (cls == 0) == (stage == 1)
        if along_x:
            at = lax.rem(x + delta, RING)
            return at, (dp, y * RING + at)
        at = lax.rem(y + delta, RING)
        return at, (dp, at * RING + x)

    def row_peer(delta):
        at = lax.rem(dp + delta, n_dp)
        return at, (at, cl)

    barrier = pltpu.get_barrier_semaphore()
    friends = [peer(cls, 1, d)[1] for cls in (0, 1) for d in range(1, RING)]
    friends += [row_peer(d)[1] for d in range(1, n_dp)]
    for friend in friends:
        pl.semaphore_signal(barrier, inc=1, device_id=friend, device_id_type=MESH)
    pl.semaphore_wait(barrier, len(friends))

    def spot(step, cls):
        row0, c0 = pieces[step]
        return pl.ds(row0 + cls * half, ROWS), pl.ds(c0, wide)

    def copies1(step, cls):
        q = 2 * step + cls
        rows, cols = spot(step, cls)
        me = x if cls == 0 else y
        return [
            pltpu.make_async_remote_copy(
                src_ref=pts.at[:, rows, cols],
                dst_ref=got1[q].at[pl.ds(me * nb, nb)],
                send_sem=s1.at[q, d - 1],
                recv_sem=r1.at[q, d - 1],
                device_id=peer(cls, 1, d)[1],
                device_id_type=MESH,
            )
            for d in range(1, RING)
        ]

    def copies2(step, cls):
        q = 2 * step + cls
        me = y if cls == 0 else x
        made = []
        for d in range(1, RING):
            at, device = peer(cls, 2, d)
            made.append(
                pltpu.make_async_remote_copy(
                    src_ref=pack2[q].at[pl.ds(at * MID_CAP, MID_CAP)],
                    dst_ref=got2[q].at[pl.ds(me * MID_CAP, MID_CAP)],
                    send_sem=s2.at[q, d - 1],
                    recv_sem=r2.at[q, d - 1],
                    device_id=device,
                    device_id_type=MESH,
                )
            )
        return made

    def copies3(step, cls):
        q = 2 * step + cls
        rows, cols = spot(step, cls)
        made = []
        for d in range(1, n_dp):
            at, device = row_peer(d)
            made.append(
                pltpu.make_async_remote_copy(
                    src_ref=pack3[q].at[pl.ds(at * OWN_CAP, OWN_CAP)],
                    dst_ref=out.at[pl.ds(dp * OWN_CAP, OWN_CAP), rows, cols],
                    send_sem=s3.at[q, d - 1],
                    recv_sem=r3.at[q, d - 1],
                    device_id=device,
                    device_id_type=MESH,
                )
            )
        return made

    def own_copy(step, cls):
        q = 2 * step + cls
        rows, cols = spot(step, cls)
        return pltpu.make_async_copy(
            pack3[q].at[pl.ds(dp * OWN_CAP, OWN_CAP)], out.at[pl.ds(dp * OWN_CAP, OWN_CAP), rows, cols], own.at[q]
        )

    def start1(step):
        for cls in (0, 1):
            for copy in copies1(step, cls):
                copy.start()

    def step12(step):
        for cls in (0, 1):
            q = 2 * step + cls
            rows, cols = spot(step, cls)
            me = x if cls == 0 else y
            mid = y if cls == 0 else x
            got1[q][pl.ds(me * nb, nb)] = pts[:, rows, cols]
            for copy in copies1(step, cls):
                copy.wait_recv()

            def pack(k, carry, q=q, cls=cls):
                pack2[q][k] = got1[q][tab[cls * RING * MID_CAP + k]]
                return carry

            lax.fori_loop(0, RING * MID_CAP, pack, 0, unroll=8)
            for copy in copies2(step, cls):
                copy.start()
            got2[q][pl.ds(mid * MID_CAP, MID_CAP)] = pack2[q][pl.ds(mid * MID_CAP, MID_CAP)]

    def step23(step):
        for cls in (0, 1):
            q = 2 * step + cls
            for copy in copies2(step, cls):
                copy.wait_recv()
            base = 2 * RING * MID_CAP + cls * n_dp * OWN_CAP

            def pack(k, carry, q=q, base=base):
                pack3[q][k] = got2[q][tab[base + k]]
                return carry

            lax.fori_loop(0, n_dp * OWN_CAP, pack, 0, unroll=8)
            for copy in copies3(step, cls):
                copy.start()
            own_copy(step, cls).start()

    start1(0)
    start1(1)
    for step in range(steps + 1):
        if step < steps:
            step12(step)
            if step + 2 < steps:
                start1(step + 2)
        if step >= 1:
            step23(step - 1)
    for step in range(steps):
        for cls in (0, 1):
            for copy in copies1(step, cls) + copies2(step, cls):
                copy.wait_send()
            for copy in copies3(step, cls):
                copy.wait()
            own_copy(step, cls).wait()


def route(points, table, n_dp):
    nb, blk, width = points.shape
    total = 2 * (blk // 2 // ROWS) * COL_SPLIT
    wide = width // COL_SPLIT
    kind = points.dtype

    def many(count):
        return [pltpu.VMEM((count, ROWS, wide), kind) for _ in range(total)]

    return pl.pallas_call(
        functools.partial(route_kernel, nb, blk, width, n_dp),
        out_shape=jax.ShapeDtypeStruct((n_dp * OWN_CAP, blk, width), kind),
        in_specs=[pl.BlockSpec(memory_space=pltpu.SMEM), pl.BlockSpec(memory_space=pltpu.VMEM)],
        out_specs=pl.BlockSpec(memory_space=pl.ANY),
        scratch_shapes=many(RING * nb) + many(RING * MID_CAP) * 2 + many(n_dp * OWN_CAP)
        + [pltpu.SemaphoreType.DMA((total, RING - 1))] * 4
        + [pltpu.SemaphoreType.DMA((total, n_dp - 1))] * 2
        + [pltpu.SemaphoreType.DMA((total,))],
        compiler_params=pltpu.CompilerParams(
            collective_id=0, has_side_effects=True, vmem_limit_bytes=60 * 1024 * 1024
        ),
        name="route",
    )(table, points)


def product_kernel(slots, cl_own, blk, tile, factor, place, blocks, train, gram, cross, sorted_blocks, scores, sem):
    group = pl.program_id(0)
    part = pl.program_id(1)
    step_rows = 2 * blk

    def fetch(k):
        at = place[k]
        return at, pltpu.make_async_copy(blocks.at[k], sorted_blocks.at[pl.ds(pl.multiple_of(at * blk, blk), blk)], sem.at[k])

    @pl.when((group == 0) & (part == 0))
    def _():
        def begin(k, carry):
            @pl.when(place[k] >= 0)
            def _():
                fetch(k)[1].start()
            return carry

        lax.fori_loop(0, slots, begin, 0)
        for owned in range(cl_own):
            count = place[slots + owned]
            end = place[slots + cl_own + owned] + count

            @pl.when(lax.rem(count, 2) == 1)
            def _():
                sorted_blocks[pl.ds(pl.multiple_of(end * blk, blk), blk), :] = jnp.zeros(
                    (blk, sorted_blocks.shape[1]), sorted_blocks.dtype
                )

        def finish(k, carry):
            @pl.when(place[k] >= 0)
            def _():
                fetch(k)[1].wait()
            return carry

        lax.fori_loop(0, slots, finish, 0)

    count = place[slots + group]
    base = place[slots + cl_own + group]
    steps = lax.div(count + 1, 2)

    def rows_of(step):
        return pl.ds(pl.multiple_of((base + 2 * step) * blk, blk), step_rows)

    @pl.when(part == 0)
    def _():
        def score(step, carry):
            rows = sorted_blocks[rows_of(step), :]
            wide = rows.astype(jnp.float32)
            weight = lax.rsqrt(jnp.mean(wide * wide, axis=1, keepdims=True) + 1e-06)
            raw = lax.dot_general(rows, train[0], (((1,), (1,)), ((), ())), preferred_element_type=jnp.float32)
            scores[pl.ds(pl.multiple_of(step * step_rows, step_rows), step_rows), :] = (raw * weight).astype(scores.dtype)
            return carry

        lax.fori_loop(0, steps, score, 0)

    columns = pl.ds(pl.multiple_of(part * tile, tile), tile)

    def terms(step):
        rows = rows_of(step)
        left = sorted_blocks[rows, columns]
        contract = (((0,), (0,)), ((), ()))
        a = lax.dot_general(left, sorted_blocks[rows, :], contract, preferred_element_type=jnp.float32)
        part_scores = scores[pl.ds(pl.multiple_of(step * step_rows, step_rows), step_rows), :]
        b = lax.dot_general(left, part_scores, contract, preferred_element_type=jnp.float32)
        return a * factor, b * factor

    @pl.when(count == 0)
    def _():
        gram[...] = jnp.zeros_like(gram)
        cross[...] = jnp.zeros_like(cross)

    @pl.when(count > 0)
    def _():
        a, b = terms(0)
        gram[0] = a
        cross[0] = b

        def add(step, carry):
            a, b = terms(step)
            gram[0] += a
            cross[0] += b
            return carry

        lax.fori_loop(1, steps, add, 0)


def products(blocks, place, train):
    slots, blk, width = blocks.shape
    cl_own, mq, _ = train.shape
    tile = 256
    return pl.pallas_call(
        functools.partial(product_kernel, slots, cl_own, blk, tile, 1.0 / MEANROWS),
        out_shape=(
            jax.ShapeDtypeStruct((cl_own, width, width), jnp.float32),
            jax.ShapeDtypeStruct((cl_own, width, mq), jnp.float32),
        ),
        grid_spec=pltpu.PrefetchScalarGridSpec(
            num_scalar_prefetch=1,
            grid=(cl_own, width // tile),
            in_specs=[
                pl.BlockSpec(memory_space=pl.ANY),
                pl.BlockSpec((1, mq, width), lambda g, i, place: (g, 0, 0)),
            ],
            out_specs=(
                pl.BlockSpec((1, tile, width), lambda g, i, place: (g, i, 0)),
                pl.BlockSpec((1, tile, mq), lambda g, i, place: (g, i, 0)),
            ),
            scratch_shapes=[
                pltpu.VMEM(((slots + cl_own) * blk, width), blocks.dtype),
                pltpu.VMEM(((slots + 2) * blk, mq), blocks.dtype),
                pltpu.SemaphoreType.DMA((slots,)),
            ],
        ),
        compiler_params=pltpu.CompilerParams(
            dimension_semantics=("arbitrary", "arbitrary"), vmem_limit_bytes=40 * 1024 * 1024
        ),
        name="products",
    )(place, blocks, train)


def local(points, block_cluster, queries, query_ids):
    n_clus = lax.axis_size("clus")
    n_dp = lax.axis_size("dp")
    dp = lax.axis_index("dp")
    cl = lax.axis_index("clus")
    nb, _, width = points.shape
    cl_own, mq = query_ids.shape
    labels = lax.all_gather(block_cluster[:, 0], ("dp", "clus"), axis=0, tiled=True).reshape(n_dp, n_clus * nb)
    table, slot_local = tables(labels, dp, cl, cl_own, n_dp, n_clus, nb)
    place = place_slots(slot_local, cl_own)
    all_queries = lax.all_gather(queries, ("dp", "clus"), axis=0, tiled=True)
    own_blocks = route(points, table, n_dp)
    train = jnp.take(all_queries, query_ids.reshape(cl_own * mq), axis=0, mode="clip").reshape(cl_own, mq, width)
    return products(own_blocks, place, train)


def solution(mesh):
    placed = (
        P(("dp", "clus"), None, None),
        P(("dp", "clus"), None),
        P(("dp", "clus"), None),
        P(("dp", "clus"), None),
    )
    return jax.shard_map(
        local,
        mesh=mesh,
        in_specs=placed,
        out_specs=(P(("dp", "clus"), None, None), P(("dp", "clus"), None, None)),
        check_vma=False,
    )
```

```python
import functools

import jax
import jax.numpy as jnp
from jax import lax
from jax.experimental import pallas as pl
from jax.experimental.pallas import tpu as pltpu
from jax.sharding import PartitionSpec as P

MEANROWS = 256
MESH = pl.DeviceIdType.MESH
RING = 4
MID_CAP = 8
OWN_CAP = 3
ROWS = 16
LANES = 128
FIRST_SPLIT = (4, 4, 2)
OTHER_SPLIT = (2, 2)


def lanes_of(shape):
    return lax.broadcasted_iota(jnp.int32, shape, 1)


def shifted(values, amount):
    return jnp.where(lanes_of(values.shape) >= amount, pltpu.roll(values, amount, axis=1), 0)


def before(mask):
    total = mask
    step = 1
    while step < LANES:
        total = total + shifted(total, step)
        step *= 2
    return total - mask


def rows_sum(values):
    return jnp.broadcast_to(jnp.sum(values, axis=1, keepdims=True), values.shape)


def tall(values, rows):
    return jnp.broadcast_to(values[0:1, :], (rows, LANES))


def route_kernel(pieces, nb, blk, width, n_dp, n_clus, cl_own, mq, *refs):
    labels, pts, queries, ids = refs[:4]
    out, place, train = refs[4:7]
    scratch = refs[7:]
    steps = len(pieces)
    total = 2 * steps
    half = blk // 2
    got1, pack2, got2, pack3 = (scratch[i * total:(i + 1) * total] for i in range(4))
    (
        s1, r1, s2, r2, s3, r3, own,
        mine, got_x, got_y, ring_label, got_r, row_label, got_d,
        tab_a, tab_b, tab_c, tab_d, sm_a, sm_b, sm_c, sm_d,
        sx, rx, sy, ry, sr, rr, sd, rd, tsem,
        q_dp, q_a, q_b, q_a2, q_b2, sq0, rq0, sqa1, rqa1, sqb1, rqb1, sqa2, rqa2, sqb2, rqb2, sq3, rq3,
        picked,
    ) = scratch[4 * total:]
    dp = lax.axis_index("dp")
    cl = lax.axis_index("clus")
    y, x = lax.div(cl, RING), lax.rem(cl, RING)
    core = lax.rem(dp, 2)
    clus_bits = n_clus.bit_length() - 1
    own_bits = cl_own.bit_length() - 1

    def along_x(delta):
        at = lax.rem(x + delta, RING)
        return at, (dp, y * RING + at)

    def along_y(delta):
        at = lax.rem(y + delta, RING)
        return at, (dp, at * RING + x)

    def peer(cls, stage, delta):
        return along_x(delta) if (cls == 0) == (stage == 1) else along_y(delta)

    def row_peer(delta):
        at = lax.rem(dp + delta, n_dp)
        return at, (at, cl)

    def send(src, dst, send_sem, recv_sem, device):
        return pltpu.make_async_remote_copy(
            src_ref=src, dst_ref=dst, send_sem=send_sem, recv_sem=recv_sem, device_id=device, device_id_type=MESH
        )

    barrier = pltpu.get_barrier_semaphore()
    friends = [along_x(d)[1] for d in range(1, RING)] + [along_y(d)[1] for d in range(1, RING)]
    friends += [row_peer(d)[1] for d in range(1, n_dp)]
    for friend in friends:
        pl.semaphore_signal(barrier, inc=1, device_id=friend, device_id_type=MESH)

    lane8 = lanes_of((8, LANES))
    vector = jnp.zeros((8, LANES), jnp.int32)
    for j in range(nb):
        vector = jnp.where(lane8 == cl * nb + j, labels[j, 0] + 1, vector)
    mine[...] = vector

    pl.semaphore_wait(barrier, len(friends))

    def spot(step, cls):
        row0, c0, wide = pieces[step]
        return pl.ds(row0 + cls * half, ROWS), pl.ds(c0, wide)

    def copies1(step, cls):
        q = 2 * step + cls
        rows, cols = spot(step, cls)
        me = x if cls == 0 else y
        return [
            send(pts.at[:, rows, cols], got1[q].at[pl.ds(me * nb, nb)], s1.at[q, d - 1], r1.at[q, d - 1], peer(cls, 1, d)[1])
            for d in range(1, RING)
        ]

    def copies2(step, cls):
        q = 2 * step + cls
        me = y if cls == 0 else x
        made = []
        for d in range(1, RING):
            at, device = peer(cls, 2, d)
            made.append(
                send(
                    pack2[q].at[pl.ds(at * MID_CAP, MID_CAP)],
                    got2[q].at[pl.ds(me * MID_CAP, MID_CAP)],
                    s2.at[q, d - 1], r2.at[q, d - 1], device,
                )
            )
        return made

    def copies3(step, cls):
        q = 2 * step + cls
        rows, cols = spot(step, cls)
        made = []
        for d in range(1, n_dp):
            at, device = row_peer(d)
            made.append(
                send(
                    pack3[q].at[pl.ds(at * OWN_CAP, OWN_CAP)],
                    out.at[pl.ds(dp * OWN_CAP, OWN_CAP), rows, cols],
                    s3.at[q, d - 1], r3.at[q, d - 1], device,
                )
            )
        return made

    def own_copy(step, cls):
        q = 2 * step + cls
        rows, cols = spot(step, cls)
        return pltpu.make_async_copy(
            pack3[q].at[pl.ds(dp * OWN_CAP, OWN_CAP)], out.at[pl.ds(dp * OWN_CAP, OWN_CAP), rows, cols], own.at[q]
        )

    def labels_x():
        return [send(mine, got_x.at[d - 1], sx.at[d - 1], rx.at[d - 1], along_x(d)[1]) for d in range(1, RING)]

    def labels_y():
        return [send(mine, got_y.at[d - 1], sy.at[d - 1], ry.at[d - 1], along_y(d)[1]) for d in range(1, RING)]

    def labels_r():
        return [send(ring_label, got_r.at[d - 1], sr.at[d - 1], rr.at[d - 1], along_y(d)[1]) for d in range(1, RING)]

    def labels_d():
        return [send(row_label, got_d.at[d - 1], sd.at[d - 1], rd.at[d - 1], row_peer(d)[1]) for d in range(1, n_dp)]

    part = width // 2
    quarter = part // 2

    def queries_dp():
        made = []
        for d in range(1, n_dp):
            at, device = row_peer(d)
            cols = pl.ds(pl.multiple_of(lax.rem(at, 2) * part, part), part)
            made.append(send(queries.at[:, cols], q_dp.at[dp], sq0.at[d - 1], rq0.at[d - 1], device))
        return made

    def queries_first():
        a = [
            send(q_dp.at[:, :, pl.ds(0, quarter)], q_a.at[y, x], sqa1.at[d - 1], rqa1.at[d - 1], along_x(d)[1])
            for d in range(1, RING)
        ]
        b = [
            send(q_dp.at[:, :, pl.ds(quarter, quarter)], q_b.at[y, x], sqb1.at[d - 1], rqb1.at[d - 1], along_y(d)[1])
            for d in range(1, RING)
        ]
        return a + b

    def queries_second():
        a = [send(q_a.at[y], q_a.at[y], sqa2.at[d - 1], rqa2.at[d - 1], along_y(d)[1]) for d in range(1, RING)]
        b = [send(q_b.at[:, x], q_b.at[:, x], sqb2.at[d - 1], rqb2.at[d - 1], along_x(d)[1]) for d in range(1, RING)]
        return a + b

    def queries_swap():
        device = (dp + 1 - 2 * core, cl)
        return [
            send(q_a, q_a2, sq3.at[0], rq3.at[0], device),
            send(q_b, q_b2, sq3.at[1], rq3.at[1], device),
        ]

    def start(copies):
        for copy in copies:
            copy.start()

    def start1(step):
        for cls in (0, 1):
            start(copies1(step, cls))

    def own1(step):
        for cls in (0, 1):
            rows, cols = spot(step, cls)
            me = x if cls == 0 else y
            got1[2 * step + cls][pl.ds(me * nb, nb)] = pts[:, rows, cols]

    def columns_of(values):
        return jnp.right_shift(values - 1, own_bits) & (n_clus - 1)

    def tables12():
        for copy in labels_x():
            copy.wait_recv()
        ring_x = mine[...]
        for d in range(1, RING):
            ring_x = ring_x + got_x[d - 1]
        ring_label[...] = ring_x
        for copy in labels_y():
            copy.wait_recv()
        ring_y = mine[...]
        for d in range(1, RING):
            ring_y = ring_y + got_y[d - 1]
        count = RING * MID_CAP
        lane = lanes_of((count, LANES))
        row = lax.broadcasted_iota(jnp.int32, (count, LANES), 0)
        peer_at, slot = jnp.right_shift(row, 3), row & (MID_CAP - 1)
        for tab, values, wanted, index in (
            (tab_a, ring_x, peer_at * RING + x, lane & (RING * nb - 1)),
            (tab_b, ring_y, y * RING + peer_at, jnp.right_shift(lane, 4) * nb + (lane & (nb - 1))),
        ):
            values = tall(values, count)
            hit = ((values > 0) & (columns_of(values) == wanted)).astype(jnp.int32)
            tab[...] = rows_sum(jnp.where((hit > 0) & (before(hit) == slot), index, 0))
        start(labels_r())
        own1(0)
        own1(1)
        for i, (tab, sm) in enumerate(((tab_a, sm_a), (tab_b, sm_b))):
            copy = pltpu.make_async_copy(tab, sm, tsem.at[i])
            copy.start()
            copy.wait()

    def tables3():
        for copy in labels_r():
            copy.wait_recv()
        row_v = ring_label[...]
        for d in range(1, RING):
            row_v = row_v + got_r[d - 1]
        row_label[...] = row_v
        hit = ((row_v > 0) & (columns_of(row_v) == cl)).astype(jnp.int32)
        lane = lane8
        inside = lane & (RING * nb - 1)
        count = hit
        step = 1
        while step < RING * nb:
            count = count + jnp.where(inside >= step, pltpu.roll(count, step, axis=1), 0)
            step *= 2
        at_a = jnp.right_shift(lane, 4) * MID_CAP + count - hit
        earlier = hit
        for step in (RING * nb, 2 * RING * nb):
            earlier = earlier + shifted(earlier, step)
        earlier = earlier - hit
        j = lane & (nb - 1)
        rank = earlier
        for step in range(1, nb):
            rank = rank + jnp.where(j >= step, pltpu.roll(earlier + hit, step, axis=1), 0)
            rank = rank + jnp.where(j < nb - step, pltpu.roll(earlier, LANES - step, axis=1), 0)
        at_b = (jnp.right_shift(lane, 2) & (RING - 1)) * MID_CAP + rank
        count = n_dp * OWN_CAP
        values = tall(row_v, count)
        row = lax.broadcasted_iota(jnp.int32, (count, LANES), 0)
        to_row, slot = row & (n_dp - 1), jnp.right_shift(row, 3)
        row_of = jnp.right_shift(values - 1, own_bits + clus_bits)
        hit = ((values > 0) & (columns_of(values) == cl) & (row_of == to_row)).astype(jnp.int32)
        chosen = (hit > 0) & (before(hit) == slot)
        tab_c[...] = rows_sum(jnp.where(chosen, tall(at_a, count), 0))
        tab_d[...] = rows_sum(jnp.where(chosen, tall(at_b, count), 0))
        start(labels_d())
        for i, (tab, sm) in enumerate(((tab_c, sm_c), (tab_d, sm_d))):
            copy = pltpu.make_async_copy(tab, sm, tsem.at[2 + i])
            copy.start()
            copy.wait()

    def place_slots():
        for copy in labels_d():
            copy.wait_recv()
        sub = lax.broadcasted_iota(jnp.int32, (n_dp, LANES), 0)
        everything = jnp.where(sub == dp, row_label[...], 0)
        for d in range(1, n_dp):
            everything = jnp.where(sub == lax.rem(dp + n_dp - d, n_dp), got_d[d - 1], everything)
        here = dp * n_clus + cl
        hit = ((everything > 0) & (jnp.right_shift(everything - 1, own_bits) == here)).astype(jnp.int32)
        rank = before(hit)
        local = ((everything - 1) & (cl_own - 1)) + 1
        kinds = [rows_sum(jnp.where((hit > 0) & (rank == k), local, 0)) for k in range(OWN_CAP)]
        positions = [jnp.full((n_dp, LANES), -1, jnp.int32) for _ in range(OWN_CAP)]
        base = jnp.zeros((n_dp, LANES), jnp.int32)
        result = jnp.zeros((n_dp, LANES), jnp.int32)
        lane = lanes_of((n_dp, LANES))
        for owned in range(cl_own):
            marks = [(kind == owned + 1).astype(jnp.int32) for kind in kinds]
            per_row = sum(marks[1:], marks[0])
            running = per_row
            step = 1
            while step < n_dp:
                running = running + jnp.where(sub >= step, pltpu.roll(running, step, axis=0), 0)
                step *= 2
            ahead = base + running - per_row
            for k in range(OWN_CAP):
                positions[k] = jnp.where(marks[k] > 0, ahead, positions[k])
                ahead = ahead + marks[k]
            count = jnp.broadcast_to(jnp.sum(per_row, axis=0, keepdims=True), (n_dp, LANES))
            result = jnp.where(lane == OWN_CAP + owned, count, result)
            result = jnp.where(lane == OWN_CAP + cl_own + owned, base, result)
            base = base + jnp.right_shift(count + 1, 1) * 2
        for k in range(OWN_CAP):
            result = jnp.where(lane == k, positions[k], result)
        place[...] = result

    def step12(step):
        for cls in (0, 1):
            q = 2 * step + cls
            mid = y if cls == 0 else x
            for copy in copies1(step, cls):
                copy.wait_recv()
            sm = (sm_a, sm_b)[cls]

            def pack(k, carry, q=q, sm=sm):
                pack2[q][k] = got1[q][sm[k, 0]]
                return carry

            lax.fori_loop(0, RING * MID_CAP, pack, 0, unroll=8)
            start(copies2(step, cls))
            got2[q][pl.ds(mid * MID_CAP, MID_CAP)] = pack2[q][pl.ds(mid * MID_CAP, MID_CAP)]

    def step23(step):
        for cls in (0, 1):
            q = 2 * step + cls
            for copy in copies2(step, cls):
                copy.wait_recv()
            sm = (sm_c, sm_d)[cls]

            def pack(d, carry, q=q, sm=sm):
                for k in range(OWN_CAP):
                    pack3[q][d * OWN_CAP + k] = got2[q][sm[k * n_dp + d, 0]]
                return carry

            lax.fori_loop(0, n_dp, pack, 0, unroll=4)
            start(copies3(step, cls))
            own_copy(step, cls).start()

    def pick_train():
        group = RING * n_dp * queries.shape[0]
        per = queries.shape[0]
        per_bits = per.bit_length() - 1
        row = lax.broadcasted_iota(jnp.int32, (group, mq), 0)
        inner = row & (n_dp * per - 1)
        at_x = jnp.right_shift(row, per_bits + 3)
        stripe = jnp.right_shift(inner, per_bits) * (n_clus * per) + at_x * per + (inner & (per - 1))
        for owned in range(cl_own):
            wanted = jnp.clip(ids[owned:owned + 1, :], 0, n_dp * n_clus * per - 1)

            def add(at_y, carry, owned=owned, wanted=wanted):
                chosen = jnp.where(stripe + at_y * (RING * per) == wanted, 1.0, 0.0).astype(queries.dtype)
                for source, side, which in ((q_a, 0, 0), (q_b, 0, 1), (q_a2, 1, 0), (q_b2, 1, 1)):
                    values = source[at_y].reshape(group, quarter)
                    term = lax.dot_general(
                        chosen, values, (((0,), (0,)), ((), ())), preferred_element_type=jnp.float32
                    )
                    picked[owned, 2 * side + which] += term
                return carry

            lax.fori_loop(0, RING, add, 0)

    start(labels_x())
    start(labels_y())
    start1(0)
    start1(1)
    start(queries_dp())
    q_dp[dp] = queries[:, pl.ds(pl.multiple_of(core * part, part), part)]
    picked[...] = jnp.zeros_like(picked)
    tables12()
    for step in range(steps + 1):
        if step < steps:
            step12(step)
            if step + 2 < steps:
                start1(step + 2)
                own1(step + 2)
        if step == 0:
            tables3()
        if step == 2:
            for copy in queries_dp():
                copy.wait_recv()
            q_a[y, x] = q_dp[:, :, pl.ds(0, quarter)]
            q_b[y, x] = q_dp[:, :, pl.ds(quarter, quarter)]
            start(queries_first())
            place_slots()
        if step == steps - 1:
            for copy in queries_first():
                copy.wait_recv()
            start(queries_second())
        if step >= 1:
            step23(step - 1)
    for copy in queries_second():
        copy.wait_recv()
    start(queries_swap())
    for copy in queries_swap():
        copy.wait_recv()
    pick_train()
    for owned in range(cl_own):
        for which in range(2):
            for side in range(2):
                at = lax.rem(core + side, 2) * part + which * quarter
                train[owned, :, pl.ds(pl.multiple_of(at, quarter), quarter)] = picked[owned, 2 * side + which].astype(
                    train.dtype
                )
    finished = labels_x() + labels_y() + labels_r() + labels_d()
    finished += queries_dp() + queries_first() + queries_second() + queries_swap()
    for step in range(steps):
        for cls in (0, 1):
            finished += copies1(step, cls) + copies2(step, cls)
    for copy in finished:
        copy.wait_send()
    for step in range(steps):
        for cls in (0, 1):
            for copy in copies3(step, cls):
                copy.wait()
            own_copy(step, cls).wait()


def route(points, block_cluster, queries, query_ids, n_dp, n_clus):
    nb, blk, width = points.shape
    cl_own, mq = query_ids.shape
    per = queries.shape[0]
    kind = points.dtype
    pieces = []
    for row0 in range(0, blk // 2, ROWS):
        at = 0
        for part in FIRST_SPLIT if row0 == 0 else OTHER_SPLIT:
            wide = width // part
            pieces.append((row0, at, wide))
            at += wide
    total = 2 * len(pieces)
    dma = pltpu.SemaphoreType.DMA

    def many(count):
        return [pltpu.VMEM((count, ROWS, wide), kind) for _, _, wide in pieces for _ in range(2)]

    def pair(*shape):
        return [dma(shape), dma(shape)]

    def ints(*shape):
        return pltpu.VMEM(shape + (LANES,), jnp.int32)

    mid_rows, own_rows = RING * MID_CAP, n_dp * OWN_CAP
    scratch = many(RING * nb) + many(RING * MID_CAP) * 2 + many(n_dp * OWN_CAP)
    scratch += pair(total, RING - 1) + pair(total, RING - 1) + pair(total, n_dp - 1) + [dma((total,))]
    scratch += [ints(8), ints(RING - 1, 8), ints(RING - 1, 8), ints(8), ints(RING - 1, 8), ints(8), ints(n_dp - 1, 8)]
    scratch += [ints(mid_rows), ints(mid_rows), ints(own_rows), ints(own_rows)]
    scratch += [pltpu.SMEM((rows, LANES), jnp.int32) for rows in (mid_rows, mid_rows, own_rows, own_rows)]
    scratch += pair(RING - 1) * 3 + pair(n_dp - 1) + [dma((4,))]
    quarter = width // 4
    scratch += [pltpu.VMEM((n_dp, per, width // 2), kind)]
    scratch += [pltpu.VMEM((RING, RING, n_dp, per, quarter), kind)] * 4
    scratch += pair(n_dp - 1) + pair(RING - 1) * 4 + pair(2)
    scratch += [pltpu.VMEM((cl_own, 4, mq, quarter), jnp.float32)]
    vmem = pl.BlockSpec(memory_space=pltpu.VMEM)
    return pl.pallas_call(
        functools.partial(route_kernel, pieces, nb, blk, width, n_dp, n_clus, cl_own, mq),
        out_shape=(
            jax.ShapeDtypeStruct((n_dp * OWN_CAP, blk, width), kind),
            jax.ShapeDtypeStruct((n_dp, LANES), jnp.int32),
            jax.ShapeDtypeStruct((cl_own, mq, width), kind),
        ),
        in_specs=[pl.BlockSpec(memory_space=pltpu.SMEM), vmem, vmem, vmem],
        out_specs=(pl.BlockSpec(memory_space=pl.ANY), vmem, vmem),
        scratch_shapes=scratch,
        compiler_params=pltpu.CompilerParams(
            collective_id=0, has_side_effects=True, vmem_limit_bytes=60 * 1024 * 1024
        ),
        name="route",
    )(block_cluster, points, queries, query_ids)


def product_kernel(slots, cl_own, blk, tile, factor, place, blocks, train, gram, cross, sorted_blocks, scores, sem):
    group = pl.program_id(0)
    part = pl.program_id(1)
    step_rows = 2 * blk

    def goal(k):
        return place[lax.div(k, OWN_CAP), lax.rem(k, OWN_CAP)]

    def fetch(k):
        rows = pl.ds(pl.multiple_of(goal(k) * blk, blk), blk)
        return pltpu.make_async_copy(blocks.at[k], sorted_blocks.at[rows], sem.at[k])

    @pl.when((group == 0) & (part == 0))
    def _():
        def begin(k, carry):
            @pl.when(goal(k) >= 0)
            def _():
                fetch(k).start()
            return carry

        lax.fori_loop(0, slots, begin, 0)
        for owned in range(cl_own):
            count = place[0, OWN_CAP + owned]
            end = place[0, OWN_CAP + cl_own + owned] + count

            @pl.when(lax.rem(count, 2) == 1)
            def _():
                sorted_blocks[pl.ds(pl.multiple_of(end * blk, blk), blk), :] = jnp.zeros(
                    (blk, sorted_blocks.shape[1]), sorted_blocks.dtype
                )

        def finish(k, carry):
            @pl.when(goal(k) >= 0)
            def _():
                fetch(k).wait()
            return carry

        lax.fori_loop(0, slots, finish, 0)

    count = place[0, OWN_CAP + group]
    base = place[0, OWN_CAP + cl_own + group]
    steps = lax.div(count + 1, 2)

    def rows_of(step):
        return pl.ds(pl.multiple_of((base + 2 * step) * blk, blk), step_rows)

    @pl.when(part == 0)
    def _():
        def score(step, carry):
            rows = sorted_blocks[rows_of(step), :]
            wide = rows.astype(jnp.float32)
            weight = lax.rsqrt(jnp.mean(wide * wide, axis=1, keepdims=True) + 1e-06)
            raw = lax.dot_general(rows, train[0], (((1,), (1,)), ((), ())), preferred_element_type=jnp.float32)
            scores[pl.ds(pl.multiple_of(step * step_rows, step_rows), step_rows), :] = (raw * weight).astype(scores.dtype)
            return carry

        lax.fori_loop(0, steps, score, 0)

    columns = pl.ds(pl.multiple_of(part * tile, tile), tile)

    def terms(step):
        rows = rows_of(step)
        left = sorted_blocks[rows, columns]
        contract = (((0,), (0,)), ((), ()))
        a = lax.dot_general(left, sorted_blocks[rows, :], contract, preferred_element_type=jnp.float32)
        part_scores = scores[pl.ds(pl.multiple_of(step * step_rows, step_rows), step_rows), :]
        b = lax.dot_general(left, part_scores, contract, preferred_element_type=jnp.float32)
        return a * factor, b * factor

    @pl.when(count == 0)
    def _():
        gram[...] = jnp.zeros_like(gram)
        cross[...] = jnp.zeros_like(cross)

    @pl.when(count > 0)
    def _():
        a, b = terms(0)
        gram[0] = a
        cross[0] = b

        def add(step, carry):
            a, b = terms(step)
            gram[0] += a
            cross[0] += b
            return carry

        lax.fori_loop(1, steps, add, 0)


def products(blocks, place, train):
    slots, blk, width = blocks.shape
    cl_own, mq, _ = train.shape
    tile = 256
    return pl.pallas_call(
        functools.partial(product_kernel, slots, cl_own, blk, tile, 1.0 / MEANROWS),
        out_shape=(
            jax.ShapeDtypeStruct((cl_own, width, width), jnp.float32),
            jax.ShapeDtypeStruct((cl_own, width, mq), jnp.float32),
        ),
        grid_spec=pltpu.PrefetchScalarGridSpec(
            num_scalar_prefetch=1,
            grid=(cl_own, width // tile),
            in_specs=[
                pl.BlockSpec(memory_space=pl.ANY),
                pl.BlockSpec((1, mq, width), lambda g, i, place: (g, 0, 0)),
            ],
            out_specs=(
                pl.BlockSpec((1, tile, width), lambda g, i, place: (g, i, 0)),
                pl.BlockSpec((1, tile, mq), lambda g, i, place: (g, i, 0)),
            ),
            scratch_shapes=[
                pltpu.VMEM(((slots + cl_own) * blk, width), blocks.dtype),
                pltpu.VMEM(((slots + 2) * blk, mq), blocks.dtype),
                pltpu.SemaphoreType.DMA((slots,)),
            ],
        ),
        compiler_params=pltpu.CompilerParams(
            dimension_semantics=("arbitrary", "arbitrary"), vmem_limit_bytes=40 * 1024 * 1024
        ),
        name="products",
    )(place, blocks, train)


def local(points, block_cluster, queries, query_ids):
    own_blocks, place, train = route(
        points, block_cluster, queries, query_ids, lax.axis_size("dp"), lax.axis_size("clus")
    )
    return products(own_blocks, place, train)


def solution(mesh):
    placed = (
        P(("dp", "clus"), None, None),
        P(("dp", "clus"), None),
        P(("dp", "clus"), None),
        P(("dp", "clus"), None),
    )
    return jax.shard_map(
        local,
        mesh=mesh,
        in_specs=placed,
        out_specs=(P(("dp", "clus"), None, None), P(("dp", "clus"), None, None)),
        check_vma=False,
    )
```

```python
import functools

import jax
import jax.numpy as jnp
from jax import lax
from jax.experimental import pallas as pl
from jax.experimental.pallas import tpu as pltpu
from jax.sharding import PartitionSpec as P

MEANROWS = 256
MESH = pl.DeviceIdType.MESH
RING = 4
AHEAD = 3
MID_CAP = 8
OWN_CAP = 3
ROWS = 16
LANES = 128
FIRST_SPLIT = (4, 4, 2)
OTHER_SPLIT = (2, 2)
LAST_SPLIT = (2, 4, 4)


def lanes_of(shape):
    return lax.broadcasted_iota(jnp.int32, shape, 1)


def shifted(values, amount):
    return jnp.where(lanes_of(values.shape) >= amount, pltpu.roll(values, amount, axis=1), 0)


def before(mask):
    total = mask
    step = 1
    while step < LANES:
        total = total + shifted(total, step)
        step *= 2
    return total - mask


def rows_sum(values):
    return jnp.broadcast_to(jnp.sum(values, axis=1, keepdims=True), values.shape)


def tall(values, rows):
    return jnp.broadcast_to(values[0:1, :], (rows, LANES))


def route_kernel(pieces, nb, blk, width, n_dp, n_clus, cl_own, mq, *refs):
    labels, pts, queries, ids = refs[:4]
    out, place, train = refs[4:7]
    scratch = refs[7:]
    steps = len(pieces)
    total = 2 * steps
    half = blk // 2
    got1, pack2, got2, pack3 = (scratch[i * total:(i + 1) * total] for i in range(4))
    (
        s1, r1, s2, r2, s3, r3, own,
        mine, got_x, got_y, ring_label, got_r, row_label, got_d,
        tab_a, tab_b, tab_c, tab_d, sm_a, sm_b, sm_c, sm_d,
        sx, rx, sy, ry, sr, rr, sd, rd, tsem,
        q_dp, q_a, q_b, q_a2, q_b2, sq0, rq0, sqa1, rqa1, sqb1, rqb1, sqa2, rqa2, sqb2, rqb2, sq3, rq3,
        picked,
    ) = scratch[4 * total:]
    dp = lax.axis_index("dp")
    cl = lax.axis_index("clus")
    y, x = lax.div(cl, RING), lax.rem(cl, RING)
    core = lax.rem(dp, 2)
    clus_bits = n_clus.bit_length() - 1
    own_bits = cl_own.bit_length() - 1

    def along_x(delta):
        at = lax.rem(x + delta, RING)
        return at, (dp, y * RING + at)

    def along_y(delta):
        at = lax.rem(y + delta, RING)
        return at, (dp, at * RING + x)

    def peer(cls, stage, delta):
        return along_x(delta) if (cls == 0) == (stage == 1) else along_y(delta)

    def row_peer(delta):
        at = lax.rem(dp + delta, n_dp)
        return at, (at, cl)

    def send(src, dst, send_sem, recv_sem, device):
        return pltpu.make_async_remote_copy(
            src_ref=src, dst_ref=dst, send_sem=send_sem, recv_sem=recv_sem, device_id=device, device_id_type=MESH
        )

    barrier = pltpu.get_barrier_semaphore()
    friends = [along_x(d)[1] for d in range(1, RING)] + [along_y(d)[1] for d in range(1, RING)]
    friends += [row_peer(d)[1] for d in range(1, n_dp)]
    for friend in friends:
        pl.semaphore_signal(barrier, inc=1, device_id=friend, device_id_type=MESH)

    lane8 = lanes_of((8, LANES))
    vector = jnp.zeros((8, LANES), jnp.int32)
    for j in range(nb):
        vector = jnp.where(lane8 == cl * nb + j, labels[0, j] + 1, vector)
    mine[...] = vector

    pl.semaphore_wait(barrier, len(friends))

    def spot(step, cls):
        row0, c0, wide = pieces[step]
        return pl.ds(row0 + cls * half, ROWS), pl.ds(c0, wide)

    def copies1(step, cls):
        q = 2 * step + cls
        rows, cols = spot(step, cls)
        me = x if cls == 0 else y
        return [
            send(pts.at[:, rows, cols], got1[q].at[pl.ds(me * nb, nb)], s1.at[q, d - 1], r1.at[q, d - 1], peer(cls, 1, d)[1])
            for d in (1, RING - 1)
        ]

    def relays1(step, cls):
        q = 2 * step + cls
        me = x if cls == 0 else y
        part = nb // 2
        made = []
        for k, d in enumerate((1, RING - 1)):
            at = pl.ds(lax.rem(me + RING - d, RING) * nb + k * part, part)
            made.append(
                send(got1[q].at[at], got1[q].at[at], s1.at[q, 1 + 2 * k], r1.at[q, 1 + 2 * k], peer(cls, 1, d)[1])
            )
        return made

    def copies2(step, cls):
        q = 2 * step + cls
        me = y if cls == 0 else x
        made = []
        for d in range(1, RING):
            at, device = peer(cls, 2, d)
            made.append(
                send(
                    pack2[q].at[pl.ds(at * MID_CAP, MID_CAP)],
                    got2[q].at[pl.ds(me * MID_CAP, MID_CAP)],
                    s2.at[q, d - 1], r2.at[q, d - 1], device,
                )
            )
        return made

    def copies3(step, cls):
        q = 2 * step + cls
        rows, cols = spot(step, cls)
        made = []
        for d in range(1, n_dp):
            at, device = row_peer(d)
            made.append(
                send(
                    pack3[q].at[pl.ds(at * OWN_CAP, OWN_CAP)],
                    out.at[pl.ds(dp * OWN_CAP, OWN_CAP), rows, cols],
                    s3.at[q, d - 1], r3.at[q, d - 1], device,
                )
            )
        return made

    def own_copy(step, cls):
        q = 2 * step + cls
        rows, cols = spot(step, cls)
        return pltpu.make_async_copy(
            pack3[q].at[pl.ds(dp * OWN_CAP, OWN_CAP)], out.at[pl.ds(dp * OWN_CAP, OWN_CAP), rows, cols], own.at[q]
        )

    def labels_x():
        return [send(mine, got_x.at[d - 1], sx.at[d - 1], rx.at[d - 1], along_x(d)[1]) for d in range(1, RING)]

    def labels_y():
        return [send(mine, got_y.at[d - 1], sy.at[d - 1], ry.at[d - 1], along_y(d)[1]) for d in range(1, RING)]

    def labels_r():
        return [send(ring_label, got_r.at[d - 1], sr.at[d - 1], rr.at[d - 1], along_y(d)[1]) for d in range(1, RING)]

    def labels_d():
        return [send(row_label, got_d.at[d - 1], sd.at[d - 1], rd.at[d - 1], row_peer(d)[1]) for d in range(1, n_dp)]

    part = width // 2
    quarter = part // 2

    def queries_dp():
        made = []
        for d in range(1, n_dp):
            at, device = row_peer(d)
            cols = pl.ds(pl.multiple_of(lax.rem(at, 2) * part, part), part)
            made.append(send(queries.at[:, cols], q_dp.at[dp], sq0.at[d - 1], rq0.at[d - 1], device))
        return made

    def queries_first():
        a = [
            send(q_dp.at[:, :, pl.ds(0, quarter)], q_a.at[y, x], sqa1.at[d - 1], rqa1.at[d - 1], along_x(d)[1])
            for d in range(1, RING)
        ]
        b = [
            send(q_dp.at[:, :, pl.ds(quarter, quarter)], q_b.at[y, x], sqb1.at[d - 1], rqb1.at[d - 1], along_y(d)[1])
            for d in range(1, RING)
        ]
        return a + b

    def queries_second():
        ends = (1, RING - 1)
        a = [send(q_a.at[y], q_a.at[y], sqa2.at[d - 1], rqa2.at[d - 1], along_y(d)[1]) for d in ends]
        b = [send(q_b.at[:, x], q_b.at[:, x], sqb2.at[d - 1], rqb2.at[d - 1], along_x(d)[1]) for d in ends]
        return a + b

    def queries_relay():
        part = RING // 2
        made = []
        for k, d in enumerate((1, RING - 1)):
            some = pl.ds(k * part, part)
            a = q_a.at[lax.rem(y + RING - d, RING), some]
            b = q_b.at[some, lax.rem(x + RING - d, RING)]
            made.append(send(a, a, sqa2.at[1 + 2 * k], rqa2.at[1 + 2 * k], along_y(d)[1]))
            made.append(send(b, b, sqb2.at[1 + 2 * k], rqb2.at[1 + 2 * k], along_x(d)[1]))
        return made

    def queries_swap():
        device = (dp + 1 - 2 * core, cl)
        return [
            send(q_a, q_a2, sq3.at[0], rq3.at[0], device),
            send(q_b, q_b2, sq3.at[1], rq3.at[1], device),
        ]

    def start(copies):
        for copy in copies:
            copy.start()

    def start1(step):
        for cls in (0, 1):
            start(copies1(step, cls))

    def relay1(step):
        for cls in (0, 1):
            for copy in copies1(step, cls):
                copy.wait_recv()
            start(relays1(step, cls))

    def own1(step):
        for cls in (0, 1):
            rows, cols = spot(step, cls)
            me = x if cls == 0 else y
            got1[2 * step + cls][pl.ds(me * nb, nb)] = pts[:, rows, cols]

    def columns_of(values):
        return jnp.right_shift(values - 1, own_bits) & (n_clus - 1)

    def tables12():
        for copy in labels_x():
            copy.wait_recv()
        ring_x = mine[...]
        for d in range(1, RING):
            ring_x = ring_x + got_x[d - 1]
        ring_label[...] = ring_x
        for copy in labels_y():
            copy.wait_recv()
        ring_y = mine[...]
        for d in range(1, RING):
            ring_y = ring_y + got_y[d - 1]
        relay1(0)
        start(labels_r())
        count = RING * MID_CAP
        lane = lanes_of((count, LANES))
        row = lax.broadcasted_iota(jnp.int32, (count, LANES), 0)
        peer_at, slot = jnp.right_shift(row, 3), row & (MID_CAP - 1)
        for tab, values, wanted, index in (
            (tab_a, ring_x, peer_at * RING + x, lane & (RING * nb - 1)),
            (tab_b, ring_y, y * RING + peer_at, jnp.right_shift(lane, 4) * nb + (lane & (nb - 1))),
        ):
            values = tall(values, count)
            hit = ((values > 0) & (columns_of(values) == wanted)).astype(jnp.int32)
            tab[...] = rows_sum(jnp.where((hit > 0) & (before(hit) == slot), index, 0))
        relay1(1)
        for step in range(AHEAD):
            own1(step)
        for copy in queries_dp():
            copy.wait_recv()
        q_a[y, x] = q_dp[:, :, pl.ds(0, quarter)]
        q_b[y, x] = q_dp[:, :, pl.ds(quarter, quarter)]
        start(queries_first())
        for i, (tab, sm) in enumerate(((tab_a, sm_a), (tab_b, sm_b))):
            copy = pltpu.make_async_copy(tab, sm, tsem.at[i])
            copy.start()
            copy.wait()

    def tables3():
        for copy in labels_r():
            copy.wait_recv()
        row_v = ring_label[...]
        for d in range(1, RING):
            row_v = row_v + got_r[d - 1]
        row_label[...] = row_v
        hit = ((row_v > 0) & (columns_of(row_v) == cl)).astype(jnp.int32)
        lane = lane8
        inside = lane & (RING * nb - 1)
        count = hit
        step = 1
        while step < RING * nb:
            count = count + jnp.where(inside >= step, pltpu.roll(count, step, axis=1), 0)
            step *= 2
        at_a = jnp.right_shift(lane, 4) * MID_CAP + count - hit
        earlier = hit
        for step in (RING * nb, 2 * RING * nb):
            earlier = earlier + shifted(earlier, step)
        earlier = earlier - hit
        j = lane & (nb - 1)
        rank = earlier
        for step in range(1, nb):
            rank = rank + jnp.where(j >= step, pltpu.roll(earlier + hit, step, axis=1), 0)
            rank = rank + jnp.where(j < nb - step, pltpu.roll(earlier, LANES - step, axis=1), 0)
        at_b = (jnp.right_shift(lane, 2) & (RING - 1)) * MID_CAP + rank
        count = n_dp * OWN_CAP
        values = tall(row_v, count)
        row = lax.broadcasted_iota(jnp.int32, (count, LANES), 0)
        to_row, slot = row & (n_dp - 1), jnp.right_shift(row, 3)
        row_of = jnp.right_shift(values - 1, own_bits + clus_bits)
        hit = ((values > 0) & (columns_of(values) == cl) & (row_of == to_row)).astype(jnp.int32)
        chosen = (hit > 0) & (before(hit) == slot)
        tab_c[...] = rows_sum(jnp.where(chosen, tall(at_a, count), 0))
        tab_d[...] = rows_sum(jnp.where(chosen, tall(at_b, count), 0))
        start(labels_d())
        for i, (tab, sm) in enumerate(((tab_c, sm_c), (tab_d, sm_d))):
            copy = pltpu.make_async_copy(tab, sm, tsem.at[2 + i])
            copy.start()
            copy.wait()

    def place_slots():
        for copy in labels_d():
            copy.wait_recv()
        sub = lax.broadcasted_iota(jnp.int32, (n_dp, LANES), 0)
        everything = jnp.where(sub == dp, row_label[...], 0)
        for d in range(1, n_dp):
            everything = jnp.where(sub == lax.rem(dp + n_dp - d, n_dp), got_d[d - 1], everything)
        here = dp * n_clus + cl
        hit = ((everything > 0) & (jnp.right_shift(everything - 1, own_bits) == here)).astype(jnp.int32)
        rank = before(hit)
        local = ((everything - 1) & (cl_own - 1)) + 1
        kinds = [rows_sum(jnp.where((hit > 0) & (rank == k), local, 0)) for k in range(OWN_CAP)]
        positions = [jnp.full((n_dp, LANES), -1, jnp.int32) for _ in range(OWN_CAP)]
        base = jnp.zeros((n_dp, LANES), jnp.int32)
        result = jnp.zeros((n_dp, LANES), jnp.int32)
        lane = lanes_of((n_dp, LANES))
        for owned in range(cl_own):
            marks = [(kind == owned + 1).astype(jnp.int32) for kind in kinds]
            per_row = sum(marks[1:], marks[0])
            running = per_row
            step = 1
            while step < n_dp:
                running = running + jnp.where(sub >= step, pltpu.roll(running, step, axis=0), 0)
                step *= 2
            ahead = base + running - per_row
            for k in range(OWN_CAP):
                positions[k] = jnp.where(marks[k] > 0, ahead, positions[k])
                ahead = ahead + marks[k]
            count = jnp.broadcast_to(jnp.sum(per_row, axis=0, keepdims=True), (n_dp, LANES))
            result = jnp.where(lane == OWN_CAP + owned, count, result)
            result = jnp.where(lane == OWN_CAP + cl_own + owned, base, result)
            base = base + jnp.right_shift(count + 1, 1) * 2
        for k in range(OWN_CAP):
            result = jnp.where(lane == k, positions[k], result)
        place[...] = result

    def step12(step):
        for cls in (0, 1):
            q = 2 * step + cls
            mid = y if cls == 0 else x
            for copy in relays1(step, cls):
                copy.wait_recv()
            sm = (sm_a, sm_b)[cls]

            def pack(k, carry, q=q, sm=sm):
                pack2[q][k] = got1[q][sm[k, 0]]
                return carry

            lax.fori_loop(0, RING * MID_CAP, pack, 0, unroll=8)
            start(copies2(step, cls))
            got2[q][pl.ds(mid * MID_CAP, MID_CAP)] = pack2[q][pl.ds(mid * MID_CAP, MID_CAP)]

    def step23(step):
        for cls in (0, 1):
            q = 2 * step + cls
            for copy in copies2(step, cls):
                copy.wait_recv()
            sm = (sm_c, sm_d)[cls]

            def pack(d, carry, q=q, sm=sm):
                for k in range(OWN_CAP):
                    pack3[q][d * OWN_CAP + k] = got2[q][sm[k * n_dp + d, 0]]
                return carry

            lax.fori_loop(0, n_dp, pack, 0, unroll=4)
            start(copies3(step, cls))
            own_copy(step, cls).start()

    def pick_train():
        group = RING * n_dp * queries.shape[0]
        per = queries.shape[0]
        per_bits = per.bit_length() - 1
        row = lax.broadcasted_iota(jnp.int32, (group, mq), 0)
        inner = row & (n_dp * per - 1)
        at_x = jnp.right_shift(row, per_bits + 3)
        stripe = jnp.right_shift(inner, per_bits) * (n_clus * per) + at_x * per + (inner & (per - 1))
        for owned in range(cl_own):
            wanted = jnp.clip(ids[owned:owned + 1, :], 0, n_dp * n_clus * per - 1)

            def add(at_y, carry, owned=owned, wanted=wanted):
                chosen = jnp.where(stripe + at_y * (RING * per) == wanted, 1.0, 0.0).astype(queries.dtype)
                for source, side, which in ((q_a, 0, 0), (q_b, 0, 1), (q_a2, 1, 0), (q_b2, 1, 1)):
                    values = source[at_y].reshape(group, quarter)
                    term = lax.dot_general(
                        chosen, values, (((0,), (0,)), ((), ())), preferred_element_type=jnp.float32
                    )
                    picked[owned, 2 * side + which] += term
                return carry

            lax.fori_loop(0, RING, add, 0)

    start(labels_x())
    start(labels_y())
    start(queries_dp())
    for step in range(AHEAD):
        start1(step)
    q_dp[dp] = queries[:, pl.ds(pl.multiple_of(core * part, part), part)]
    picked[...] = jnp.zeros_like(picked)
    tables12()
    for step in range(steps + 1):
        if step < steps:
            step12(step)
            if step + 2 < steps:
                relay1(step + 2)
            if step + AHEAD < steps:
                start1(step + AHEAD)
                own1(step + AHEAD)
        if step == 0:
            tables3()
        if step == 2:
            place_slots()
        if step == steps - 5:
            for copy in queries_first():
                copy.wait_recv()
            start(queries_second())
        if step == steps - 4:
            for copy in queries_second():
                copy.wait_recv()
            start(queries_relay())
        if step == steps - 2:
            for copy in queries_relay():
                copy.wait_recv()
            start(queries_swap())
        if step >= 1:
            step23(step - 1)
    for copy in queries_swap():
        copy.wait_recv()
    pick_train()
    for owned in range(cl_own):
        for which in range(2):
            for side in range(2):
                at = lax.rem(core + side, 2) * part + which * quarter
                train[owned, :, pl.ds(pl.multiple_of(at, quarter), quarter)] = picked[owned, 2 * side + which].astype(
                    train.dtype
                )
    finished = labels_x() + labels_y() + labels_r() + labels_d()
    finished += queries_dp() + queries_first() + queries_second() + queries_relay() + queries_swap()
    for step in range(steps):
        for cls in (0, 1):
            finished += copies1(step, cls) + relays1(step, cls) + copies2(step, cls)
    for copy in finished:
        copy.wait_send()
    for step in range(steps):
        for cls in (0, 1):
            for copy in copies3(step, cls):
                copy.wait()
            own_copy(step, cls).wait()


def route(points, block_cluster, queries, query_ids, n_dp, n_clus):
    nb, blk, width = points.shape
    cl_own, mq = query_ids.shape
    per = queries.shape[0]
    kind = points.dtype
    pieces = []
    for row0 in range(0, blk // 2, ROWS):
        at = 0
        last = row0 + ROWS == blk // 2
        for part in FIRST_SPLIT if row0 == 0 else LAST_SPLIT if last else OTHER_SPLIT:
            wide = width // part
            pieces.append((row0, at, wide))
            at += wide
    total = 2 * len(pieces)
    dma = pltpu.SemaphoreType.DMA

    def many(count):
        return [pltpu.VMEM((count, ROWS, wide), kind) for _, _, wide in pieces for _ in range(2)]

    def pair(*shape):
        return [dma(shape), dma(shape)]

    def ints(*shape):
        return pltpu.VMEM(shape + (LANES,), jnp.int32)

    mid_rows, own_rows = RING * MID_CAP, n_dp * OWN_CAP
    scratch = many(RING * nb) + many(RING * MID_CAP) * 2 + many(n_dp * OWN_CAP)
    scratch += pair(total, RING) + pair(total, RING - 1) + pair(total, n_dp - 1) + [dma((total,))]
    scratch += [ints(8), ints(RING - 1, 8), ints(RING - 1, 8), ints(8), ints(RING - 1, 8), ints(8), ints(n_dp - 1, 8)]
    scratch += [ints(mid_rows), ints(mid_rows), ints(own_rows), ints(own_rows)]
    scratch += [pltpu.SMEM((rows, LANES), jnp.int32) for rows in (mid_rows, mid_rows, own_rows, own_rows)]
    scratch += pair(RING - 1) * 3 + pair(n_dp - 1) + [dma((4,))]
    quarter = width // 4
    scratch += [pltpu.VMEM((n_dp, per, width // 2), kind)]
    scratch += [pltpu.VMEM((RING, RING, n_dp, per, quarter), kind)] * 4
    scratch += pair(n_dp - 1) + pair(RING - 1) * 2 + pair(RING) * 2 + pair(2)
    scratch += [pltpu.VMEM((cl_own, 4, mq, quarter), jnp.float32)]
    vmem = pl.BlockSpec(memory_space=pltpu.VMEM)
    return pl.pallas_call(
        functools.partial(route_kernel, pieces, nb, blk, width, n_dp, n_clus, cl_own, mq),
        out_shape=(
            jax.ShapeDtypeStruct((n_dp * OWN_CAP, blk, width), kind),
            jax.ShapeDtypeStruct((n_dp, LANES), jnp.int32),
            jax.ShapeDtypeStruct((cl_own, mq, width), kind),
        ),
        in_specs=[pl.BlockSpec(memory_space=pltpu.SMEM), vmem, vmem, vmem],
        out_specs=(pl.BlockSpec(memory_space=pl.ANY), vmem, vmem),
        scratch_shapes=scratch,
        compiler_params=pltpu.CompilerParams(
            collective_id=0, has_side_effects=True, vmem_limit_bytes=60 * 1024 * 1024
        ),
        name="route",
    )(block_cluster.reshape(1, nb), points, queries, query_ids)


def product_kernel(slots, cl_own, blk, tile, factor, place, blocks, train, gram, cross, sorted_blocks, scores, sem):
    group = pl.program_id(0)
    part = pl.program_id(1)
    step_rows = 2 * blk

    def goal(k):
        return place[lax.div(k, OWN_CAP), lax.rem(k, OWN_CAP)]

    def fetch(k):
        rows = pl.ds(pl.multiple_of(goal(k) * blk, blk), blk)
        return pltpu.make_async_copy(blocks.at[k], sorted_blocks.at[rows], sem.at[k])

    @pl.when((group == 0) & (part == 0))
    def _():
        def begin(k, carry):
            @pl.when(goal(k) >= 0)
            def _():
                fetch(k).start()
            return carry

        lax.fori_loop(0, slots, begin, 0)
        for owned in range(cl_own):
            count = place[0, OWN_CAP + owned]
            end = place[0, OWN_CAP + cl_own + owned] + count

            @pl.when(lax.rem(count, 2) == 1)
            def _():
                sorted_blocks[pl.ds(pl.multiple_of(end * blk, blk), blk), :] = jnp.zeros(
                    (blk, sorted_blocks.shape[1]), sorted_blocks.dtype
                )

        def finish(k, carry):
            @pl.when(goal(k) >= 0)
            def _():
                fetch(k).wait()
            return carry

        lax.fori_loop(0, slots, finish, 0)

    count = place[0, OWN_CAP + group]
    base = place[0, OWN_CAP + cl_own + group]
    steps = lax.div(count + 1, 2)

    def rows_of(step):
        return pl.ds(pl.multiple_of((base + 2 * step) * blk, blk), step_rows)

    @pl.when(part == 0)
    def _():
        def score(step, carry):
            rows = sorted_blocks[rows_of(step), :]
            wide = rows.astype(jnp.float32)
            weight = lax.rsqrt(jnp.mean(wide * wide, axis=1, keepdims=True) + 1e-06)
            raw = lax.dot_general(rows, train[0], (((1,), (1,)), ((), ())), preferred_element_type=jnp.float32)
            scores[pl.ds(pl.multiple_of(step * step_rows, step_rows), step_rows), :] = (raw * weight).astype(scores.dtype)
            return carry

        lax.fori_loop(0, steps, score, 0)

    columns = pl.ds(pl.multiple_of(part * tile, tile), tile)

    def terms(step):
        rows = rows_of(step)
        left = sorted_blocks[rows, columns]
        contract = (((0,), (0,)), ((), ()))
        a = lax.dot_general(left, sorted_blocks[rows, :], contract, preferred_element_type=jnp.float32)
        part_scores = scores[pl.ds(pl.multiple_of(step * step_rows, step_rows), step_rows), :]
        b = lax.dot_general(left, part_scores, contract, preferred_element_type=jnp.float32)
        return a * factor, b * factor

    @pl.when(count == 0)
    def _():
        gram[...] = jnp.zeros_like(gram)
        cross[...] = jnp.zeros_like(cross)

    @pl.when(count > 0)
    def _():
        a, b = terms(0)
        gram[0] = a
        cross[0] = b

        def add(step, carry):
            a, b = terms(step)
            gram[0] += a
            cross[0] += b
            return carry

        lax.fori_loop(1, steps, add, 0)


def products(blocks, place, train):
    slots, blk, width = blocks.shape
    cl_own, mq, _ = train.shape
    tile = 256
    return pl.pallas_call(
        functools.partial(product_kernel, slots, cl_own, blk, tile, 1.0 / MEANROWS),
        out_shape=(
            jax.ShapeDtypeStruct((cl_own, width, width), jnp.float32),
            jax.ShapeDtypeStruct((cl_own, width, mq), jnp.float32),
        ),
        grid_spec=pltpu.PrefetchScalarGridSpec(
            num_scalar_prefetch=1,
            grid=(cl_own, width // tile),
            in_specs=[
                pl.BlockSpec(memory_space=pl.ANY),
                pl.BlockSpec((1, mq, width), lambda g, i, place: (g, 0, 0)),
            ],
            out_specs=(
                pl.BlockSpec((1, tile, width), lambda g, i, place: (g, i, 0)),
                pl.BlockSpec((1, tile, mq), lambda g, i, place: (g, i, 0)),
            ),
            scratch_shapes=[
                pltpu.VMEM(((slots + cl_own) * blk, width), blocks.dtype),
                pltpu.VMEM(((slots + 2) * blk, mq), blocks.dtype),
                pltpu.SemaphoreType.DMA((slots,)),
            ],
        ),
        compiler_params=pltpu.CompilerParams(
            dimension_semantics=("arbitrary", "arbitrary"), vmem_limit_bytes=60 * 1024 * 1024
        ),
        name="products",
    )(place, blocks, train)


def local(points, block_cluster, queries, query_ids):
    own_blocks, place, train = route(
        points, block_cluster, queries, query_ids, lax.axis_size("dp"), lax.axis_size("clus")
    )
    return products(own_blocks, place, train)


def solution(mesh):
    placed = (
        P(("dp", "clus"), None, None),
        P(("dp", "clus"), None),
        P(("dp", "clus"), None),
        P(("dp", "clus"), None),
    )
    return jax.shard_map(
        local,
        mesh=mesh,
        in_specs=placed,
        out_specs=(P(("dp", "clus"), None, None), P(("dp", "clus"), None, None)),
        check_vma=False,
    )
```

```python
import functools

import jax
import jax.numpy as jnp
from jax import lax
from jax.experimental import pallas as pl
from jax.experimental.pallas import tpu as pltpu
from jax.sharding import PartitionSpec as P

MEANROWS = 256
MESH = pl.DeviceIdType.MESH
RING = 4
AHEAD = 3
MID_CAP = 8
OWN_CAP = 3
ROWS = 16
LANES = 128
FIRST_SPLIT = (8, 8, 4, 2)
OTHER_SPLIT = (2, 2)
LAST_SPLIT = (2, 4, 4)


def lanes_of(shape):
    return lax.broadcasted_iota(jnp.int32, shape, 1)


def shifted(values, amount):
    return jnp.where(lanes_of(values.shape) >= amount, pltpu.roll(values, amount, axis=1), 0)


def before(mask):
    total = mask
    step = 1
    while step < LANES:
        total = total + shifted(total, step)
        step *= 2
    return total - mask


def rows_sum(values):
    return jnp.broadcast_to(jnp.sum(values, axis=1, keepdims=True), values.shape)


def tall(values, rows):
    return jnp.broadcast_to(values[0:1, :], (rows, LANES))


def route_kernel(pieces, nb, blk, width, n_dp, n_clus, cl_own, mq, *refs):
    labels, pts, queries, ids = refs[:4]
    out, place, train = refs[4:7]
    scratch = refs[7:]
    steps = len(pieces)
    total = 2 * steps
    half = blk // 2
    got1, pack2, got2, pack3 = (scratch[i * total:(i + 1) * total] for i in range(4))
    (
        s1, r1, s2, r2, s3, r3, own,
        mine, got_x, got_y, ring_label, got_r, row_label, got_d,
        tab_a, tab_b, tab_c, tab_d, sm_a, sm_b, sm_c, sm_d,
        sx, rx, sy, ry, sr, rr, sd, rd, tsem,
        q_dp, q_a, q_b, q_a2, q_b2, sq0, rq0, sqa1, rqa1, sqb1, rqb1, sqa2, rqa2, sqb2, rqb2, sq3, rq3,
        picked,
    ) = scratch[4 * total:]
    dp = lax.axis_index("dp")
    cl = lax.axis_index("clus")
    y, x = lax.div(cl, RING), lax.rem(cl, RING)
    core = lax.rem(dp, 2)
    clus_bits = n_clus.bit_length() - 1
    own_bits = cl_own.bit_length() - 1

    def along_x(delta):
        at = lax.rem(x + delta, RING)
        return at, (dp, y * RING + at)

    def along_y(delta):
        at = lax.rem(y + delta, RING)
        return at, (dp, at * RING + x)

    def peer(cls, stage, delta):
        return along_x(delta) if (cls == 0) == (stage == 1) else along_y(delta)

    def row_peer(delta):
        at = lax.rem(dp + delta, n_dp)
        return at, (at, cl)

    def send(src, dst, send_sem, recv_sem, device):
        return pltpu.make_async_remote_copy(
            src_ref=src, dst_ref=dst, send_sem=send_sem, recv_sem=recv_sem, device_id=device, device_id_type=MESH
        )

    barrier = pltpu.get_barrier_semaphore()
    friends = [along_x(d)[1] for d in range(1, RING)] + [along_y(d)[1] for d in range(1, RING)]
    friends += [row_peer(d)[1] for d in range(1, n_dp)]
    for friend in friends:
        pl.semaphore_signal(barrier, inc=1, device_id=friend, device_id_type=MESH)

    lane8 = lanes_of((8, LANES))
    vector = jnp.zeros((8, LANES), jnp.int32)
    for j in range(nb):
        vector = jnp.where(lane8 == cl * nb + j, labels[0, j] + 1, vector)
    mine[...] = vector

    pl.semaphore_wait(barrier, len(friends))

    def spot(step, cls):
        row0, c0, wide = pieces[step]
        return pl.ds(row0 + cls * half, ROWS), pl.ds(c0, wide)

    def copies1(step, cls):
        q = 2 * step + cls
        rows, cols = spot(step, cls)
        me = x if cls == 0 else y
        return [
            send(pts.at[:, rows, cols], got1[q].at[pl.ds(me * nb, nb)], s1.at[q, d - 1], r1.at[q, d - 1], peer(cls, 1, d)[1])
            for d in (1, RING - 1)
        ]

    def relays1(step, cls):
        q = 2 * step + cls
        me = x if cls == 0 else y
        part = nb // 2
        made = []
        for k, d in enumerate((1, RING - 1)):
            at = pl.ds(lax.rem(me + RING - d, RING) * nb + k * part, part)
            made.append(
                send(got1[q].at[at], got1[q].at[at], s1.at[q, 1 + 2 * k], r1.at[q, 1 + 2 * k], peer(cls, 1, d)[1])
            )
        return made

    def copies2(step, cls):
        q = 2 * step + cls
        me = y if cls == 0 else x
        made = []
        for d in range(1, RING):
            at, device = peer(cls, 2, d)
            made.append(
                send(
                    pack2[q].at[pl.ds(at * MID_CAP, MID_CAP)],
                    got2[q].at[pl.ds(me * MID_CAP, MID_CAP)],
                    s2.at[q, d - 1], r2.at[q, d - 1], device,
                )
            )
        return made

    def copies3(step, cls):
        q = 2 * step + cls
        rows, cols = spot(step, cls)
        made = []
        for d in range(1, n_dp):
            at, device = row_peer(d)
            made.append(
                send(
                    pack3[q].at[pl.ds(at * OWN_CAP, OWN_CAP)],
                    out.at[pl.ds(dp * OWN_CAP, OWN_CAP), rows, cols],
                    s3.at[q, d - 1], r3.at[q, d - 1], device,
                )
            )
        return made

    def own_copy(step, cls):
        q = 2 * step + cls
        rows, cols = spot(step, cls)
        return pltpu.make_async_copy(
            pack3[q].at[pl.ds(dp * OWN_CAP, OWN_CAP)], out.at[pl.ds(dp * OWN_CAP, OWN_CAP), rows, cols], own.at[q]
        )

    def labels_x():
        return [send(mine, got_x.at[d - 1], sx.at[d - 1], rx.at[d - 1], along_x(d)[1]) for d in range(1, RING)]

    def labels_y():
        return [send(mine, got_y.at[d - 1], sy.at[d - 1], ry.at[d - 1], along_y(d)[1]) for d in range(1, RING)]

    def labels_r():
        return [send(ring_label, got_r.at[d - 1], sr.at[d - 1], rr.at[d - 1], along_y(d)[1]) for d in range(1, RING)]

    def labels_d():
        return [send(row_label, got_d.at[d - 1], sd.at[d - 1], rd.at[d - 1], row_peer(d)[1]) for d in range(1, n_dp)]

    part = width // 2
    quarter = part // 2

    def queries_dp():
        made = []
        for d in range(1, n_dp):
            at, device = row_peer(d)
            cols = pl.ds(pl.multiple_of(lax.rem(at, 2) * part, part), part)
            made.append(send(queries.at[:, cols], q_dp.at[dp], sq0.at[d - 1], rq0.at[d - 1], device))
        return made

    def queries_first():
        a = [
            send(q_dp.at[:, :, pl.ds(0, quarter)], q_a.at[y, x], sqa1.at[d - 1], rqa1.at[d - 1], along_x(d)[1])
            for d in range(1, RING)
        ]
        b = [
            send(q_dp.at[:, :, pl.ds(quarter, quarter)], q_b.at[y, x], sqb1.at[d - 1], rqb1.at[d - 1], along_y(d)[1])
            for d in range(1, RING)
        ]
        return a + b

    def queries_second():
        ends = (1, RING - 1)
        a = [send(q_a.at[y], q_a.at[y], sqa2.at[d - 1], rqa2.at[d - 1], along_y(d)[1]) for d in ends]
        b = [send(q_b.at[:, x], q_b.at[:, x], sqb2.at[d - 1], rqb2.at[d - 1], along_x(d)[1]) for d in ends]
        return a + b

    def queries_relay():
        part = RING // 2
        made = []
        for k, d in enumerate((1, RING - 1)):
            some = pl.ds(k * part, part)
            a = q_a.at[lax.rem(y + RING - d, RING), some]
            b = q_b.at[some, lax.rem(x + RING - d, RING)]
            made.append(send(a, a, sqa2.at[1 + 2 * k], rqa2.at[1 + 2 * k], along_y(d)[1]))
            made.append(send(b, b, sqb2.at[1 + 2 * k], rqb2.at[1 + 2 * k], along_x(d)[1]))
        return made

    def queries_swap():
        device = (dp + 1 - 2 * core, cl)
        return [
            send(q_a, q_a2, sq3.at[0], rq3.at[0], device),
            send(q_b, q_b2, sq3.at[1], rq3.at[1], device),
        ]

    def start(copies):
        for copy in copies:
            copy.start()

    def start1(step):
        for cls in (0, 1):
            start(copies1(step, cls))

    def relay1(step):
        for cls in (0, 1):
            for copy in copies1(step, cls):
                copy.wait_recv()
            start(relays1(step, cls))

    def own1(step):
        for cls in (0, 1):
            rows, cols = spot(step, cls)
            me = x if cls == 0 else y
            got1[2 * step + cls][pl.ds(me * nb, nb)] = pts[:, rows, cols]

    def columns_of(values):
        return jnp.right_shift(values - 1, own_bits) & (n_clus - 1)

    def to_scalars(at, first, first_out, second, second_out):
        copies = [
            pltpu.make_async_copy(first, first_out, tsem.at[at]),
            pltpu.make_async_copy(second, second_out, tsem.at[at + 1]),
        ]
        start(copies)
        for copy in copies:
            copy.wait()

    def tables12():
        for copy in labels_x():
            copy.wait_recv()
        ring_x = mine[...]
        for d in range(1, RING):
            ring_x = ring_x + got_x[d - 1]
        ring_label[...] = ring_x
        for copy in labels_y():
            copy.wait_recv()
        ring_y = mine[...]
        for d in range(1, RING):
            ring_y = ring_y + got_y[d - 1]
        relay1(0)
        start(labels_r())
        count = RING * MID_CAP
        lane = lanes_of((count, LANES))
        row = lax.broadcasted_iota(jnp.int32, (count, LANES), 0)
        peer_at, slot = jnp.right_shift(row, 3), row & (MID_CAP - 1)
        for tab, values, wanted, index in (
            (tab_a, ring_x, peer_at * RING + x, lane & (RING * nb - 1)),
            (tab_b, ring_y, y * RING + peer_at, jnp.right_shift(lane, 4) * nb + (lane & (nb - 1))),
        ):
            values = tall(values, count)
            hit = ((values > 0) & (columns_of(values) == wanted)).astype(jnp.int32)
            tab[...] = rows_sum(jnp.where((hit > 0) & (before(hit) == slot), index, 0))
        relay1(1)
        for step in range(AHEAD):
            own1(step)
        to_scalars(0, tab_a, sm_a, tab_b, sm_b)

    def tables3():
        for copy in labels_r():
            copy.wait_recv()
        row_v = ring_label[...]
        for d in range(1, RING):
            row_v = row_v + got_r[d - 1]
        row_label[...] = row_v
        hit = ((row_v > 0) & (columns_of(row_v) == cl)).astype(jnp.int32)
        lane = lane8
        inside = lane & (RING * nb - 1)
        count = hit
        step = 1
        while step < RING * nb:
            count = count + jnp.where(inside >= step, pltpu.roll(count, step, axis=1), 0)
            step *= 2
        at_a = jnp.right_shift(lane, 4) * MID_CAP + count - hit
        earlier = hit
        for step in (RING * nb, 2 * RING * nb):
            earlier = earlier + shifted(earlier, step)
        earlier = earlier - hit
        j = lane & (nb - 1)
        rank = earlier
        for step in range(1, nb):
            rank = rank + jnp.where(j >= step, pltpu.roll(earlier + hit, step, axis=1), 0)
            rank = rank + jnp.where(j < nb - step, pltpu.roll(earlier, LANES - step, axis=1), 0)
        at_b = (jnp.right_shift(lane, 2) & (RING - 1)) * MID_CAP + rank
        count = n_dp * OWN_CAP
        values = tall(row_v, count)
        row = lax.broadcasted_iota(jnp.int32, (count, LANES), 0)
        to_row, slot = row & (n_dp - 1), jnp.right_shift(row, 3)
        row_of = jnp.right_shift(values - 1, own_bits + clus_bits)
        hit = ((values > 0) & (columns_of(values) == cl) & (row_of == to_row)).astype(jnp.int32)
        chosen = (hit > 0) & (before(hit) == slot)
        tab_c[...] = rows_sum(jnp.where(chosen, tall(at_a, count), 0))
        tab_d[...] = rows_sum(jnp.where(chosen, tall(at_b, count), 0))
        start(labels_d())
        to_scalars(2, tab_c, sm_c, tab_d, sm_d)

    def place_slots():
        for copy in labels_d():
            copy.wait_recv()
        sub = lax.broadcasted_iota(jnp.int32, (n_dp, LANES), 0)
        everything = jnp.where(sub == dp, row_label[...], 0)
        for d in range(1, n_dp):
            everything = jnp.where(sub == lax.rem(dp + n_dp - d, n_dp), got_d[d - 1], everything)
        here = dp * n_clus + cl
        hit = ((everything > 0) & (jnp.right_shift(everything - 1, own_bits) == here)).astype(jnp.int32)
        rank = before(hit)
        local = ((everything - 1) & (cl_own - 1)) + 1
        kinds = [rows_sum(jnp.where((hit > 0) & (rank == k), local, 0)) for k in range(OWN_CAP)]
        positions = [jnp.full((n_dp, LANES), -1, jnp.int32) for _ in range(OWN_CAP)]
        base = jnp.zeros((n_dp, LANES), jnp.int32)
        result = jnp.zeros((n_dp, LANES), jnp.int32)
        lane = lanes_of((n_dp, LANES))
        for owned in range(cl_own):
            marks = [(kind == owned + 1).astype(jnp.int32) for kind in kinds]
            per_row = sum(marks[1:], marks[0])
            running = per_row
            step = 1
            while step < n_dp:
                running = running + jnp.where(sub >= step, pltpu.roll(running, step, axis=0), 0)
                step *= 2
            ahead = base + running - per_row
            for k in range(OWN_CAP):
                positions[k] = jnp.where(marks[k] > 0, ahead, positions[k])
                ahead = ahead + marks[k]
            count = jnp.broadcast_to(jnp.sum(per_row, axis=0, keepdims=True), (n_dp, LANES))
            result = jnp.where(lane == OWN_CAP + owned, count, result)
            result = jnp.where(lane == OWN_CAP + cl_own + owned, base, result)
            base = base + jnp.right_shift(count + 1, 1) * 2
        for k in range(OWN_CAP):
            result = jnp.where(lane == k, positions[k], result)
        place[...] = result

    def step12(step):
        for cls in (0, 1):
            q = 2 * step + cls
            mid = y if cls == 0 else x
            for copy in relays1(step, cls):
                copy.wait_recv()
            sm = (sm_a, sm_b)[cls]

            def pack(k, carry, q=q, sm=sm):
                pack2[q][k] = got1[q][sm[k, 0]]
                return carry

            lax.fori_loop(0, RING * MID_CAP, pack, 0, unroll=8)
            start(copies2(step, cls))
            got2[q][pl.ds(mid * MID_CAP, MID_CAP)] = pack2[q][pl.ds(mid * MID_CAP, MID_CAP)]

    def step23(step):
        for cls in (0, 1):
            q = 2 * step + cls
            for copy in copies2(step, cls):
                copy.wait_recv()
            sm = (sm_c, sm_d)[cls]

            def pack(d, carry, q=q, sm=sm):
                for k in range(OWN_CAP):
                    pack3[q][d * OWN_CAP + k] = got2[q][sm[k * n_dp + d, 0]]
                return carry

            lax.fori_loop(0, n_dp, pack, 0, unroll=4)
            start(copies3(step, cls))
            own_copy(step, cls).start()

    def pick_train():
        group = RING * n_dp * queries.shape[0]
        per = queries.shape[0]
        per_bits = per.bit_length() - 1
        row = lax.broadcasted_iota(jnp.int32, (group, mq), 0)
        inner = row & (n_dp * per - 1)
        at_x = jnp.right_shift(row, per_bits + 3)
        stripe = jnp.right_shift(inner, per_bits) * (n_clus * per) + at_x * per + (inner & (per - 1))
        for owned in range(cl_own):
            wanted = jnp.clip(ids[owned:owned + 1, :], 0, n_dp * n_clus * per - 1)

            def add(at_y, carry, owned=owned, wanted=wanted):
                chosen = jnp.where(stripe + at_y * (RING * per) == wanted, 1.0, 0.0).astype(queries.dtype)
                for source, side, which in ((q_a, 0, 0), (q_b, 0, 1), (q_a2, 1, 0), (q_b2, 1, 1)):
                    values = source[at_y].reshape(group, quarter)
                    term = lax.dot_general(
                        chosen, values, (((0,), (0,)), ((), ())), preferred_element_type=jnp.float32
                    )
                    picked[owned, 2 * side + which] += term
                return carry

            lax.fori_loop(0, RING, add, 0)

    start(labels_x())
    start(labels_y())
    start(queries_dp())
    for step in range(AHEAD):
        start1(step)
    q_dp[dp] = queries[:, pl.ds(pl.multiple_of(core * part, part), part)]
    picked[...] = jnp.zeros_like(picked)
    tables12()
    for step in range(steps + 1):
        if step < steps:
            step12(step)
        if step >= 1:
            step23(step - 1)
        if step + 2 < steps:
            relay1(step + 2)
        if step + AHEAD < steps:
            start1(step + AHEAD)
            own1(step + AHEAD)
        if step == 0:
            tables3()
        if step == 1:
            for copy in queries_dp():
                copy.wait_recv()
            q_a[y, x] = q_dp[:, :, pl.ds(0, quarter)]
            q_b[y, x] = q_dp[:, :, pl.ds(quarter, quarter)]
            start(queries_first())
        if step == steps - 5:
            for copy in queries_first():
                copy.wait_recv()
            start(queries_second())
        if step == steps - 4:
            for copy in queries_second():
                copy.wait_recv()
            start(queries_relay())
        if step == steps - 3:
            place_slots()
        if step == steps - 2:
            for copy in queries_relay():
                copy.wait_recv()
            start(queries_swap())
    for copy in queries_swap():
        copy.wait_recv()
    pick_train()
    for owned in range(cl_own):
        for which in range(2):
            for side in range(2):
                at = lax.rem(core + side, 2) * part + which * quarter
                train[owned, :, pl.ds(pl.multiple_of(at, quarter), quarter)] = picked[owned, 2 * side + which].astype(
                    train.dtype
                )
    finished = labels_x() + labels_y() + labels_r() + labels_d()
    finished += queries_dp() + queries_first() + queries_second() + queries_relay() + queries_swap()
    for step in range(steps):
        for cls in (0, 1):
            finished += copies1(step, cls) + relays1(step, cls) + copies2(step, cls)
    for copy in finished:
        copy.wait_send()
    for step in range(steps):
        for cls in (0, 1):
            for copy in copies3(step, cls):
                copy.wait()
            own_copy(step, cls).wait()


def route(points, block_cluster, queries, query_ids, n_dp, n_clus):
    nb, blk, width = points.shape
    cl_own, mq = query_ids.shape
    per = queries.shape[0]
    kind = points.dtype
    pieces = []
    for row0 in range(0, blk // 2, ROWS):
        at = 0
        last = row0 + ROWS == blk // 2
        for part in FIRST_SPLIT if row0 == 0 else LAST_SPLIT if last else OTHER_SPLIT:
            wide = width // part
            pieces.append((row0, at, wide))
            at += wide
    total = 2 * len(pieces)
    dma = pltpu.SemaphoreType.DMA

    def many(count):
        return [pltpu.VMEM((count, ROWS, wide), kind) for _, _, wide in pieces for _ in range(2)]

    def pair(*shape):
        return [dma(shape), dma(shape)]

    def ints(*shape):
        return pltpu.VMEM(shape + (LANES,), jnp.int32)

    mid_rows, own_rows = RING * MID_CAP, n_dp * OWN_CAP
    scratch = many(RING * nb) + many(RING * MID_CAP) * 2 + many(n_dp * OWN_CAP)
    scratch += pair(total, RING) + pair(total, RING - 1) + pair(total, n_dp - 1) + [dma((total,))]
    scratch += [ints(8), ints(RING - 1, 8), ints(RING - 1, 8), ints(8), ints(RING - 1, 8), ints(8), ints(n_dp - 1, 8)]
    scratch += [ints(mid_rows), ints(mid_rows), ints(own_rows), ints(own_rows)]
    scratch += [pltpu.SMEM((rows, LANES), jnp.int32) for rows in (mid_rows, mid_rows, own_rows, own_rows)]
    scratch += pair(RING - 1) * 3 + pair(n_dp - 1) + [dma((4,))]
    quarter = width // 4
    scratch += [pltpu.VMEM((n_dp, per, width // 2), kind)]
    scratch += [pltpu.VMEM((RING, RING, n_dp, per, quarter), kind)] * 4
    scratch += pair(n_dp - 1) + pair(RING - 1) * 2 + pair(RING) * 2 + pair(2)
    scratch += [pltpu.VMEM((cl_own, 4, mq, quarter), jnp.float32)]
    vmem = pl.BlockSpec(memory_space=pltpu.VMEM)
    return pl.pallas_call(
        functools.partial(route_kernel, pieces, nb, blk, width, n_dp, n_clus, cl_own, mq),
        out_shape=(
            jax.ShapeDtypeStruct((n_dp * OWN_CAP, blk, width), kind),
            jax.ShapeDtypeStruct((n_dp, LANES), jnp.int32),
            jax.ShapeDtypeStruct((cl_own, mq, width), kind),
        ),
        in_specs=[pl.BlockSpec(memory_space=pltpu.SMEM), vmem, vmem, vmem],
        out_specs=(pl.BlockSpec(memory_space=pl.ANY), vmem, vmem),
        scratch_shapes=scratch,
        compiler_params=pltpu.CompilerParams(
            collective_id=0, has_side_effects=True, vmem_limit_bytes=60 * 1024 * 1024
        ),
        name="route",
    )(block_cluster.reshape(1, nb), points, queries, query_ids)


def product_kernel(slots, cl_own, blk, tile, factor, place, blocks, train, gram, cross, sorted_blocks, scores, sem):
    group = pl.program_id(0)
    part = pl.program_id(1)
    step_rows = 2 * blk

    def goal(k):
        return place[lax.div(k, OWN_CAP), lax.rem(k, OWN_CAP)]

    def fetch(k):
        rows = pl.ds(pl.multiple_of(goal(k) * blk, blk), blk)
        return pltpu.make_async_copy(blocks.at[k], sorted_blocks.at[rows], sem.at[k])

    @pl.when((group == 0) & (part == 0))
    def _():
        def begin(k, carry):
            @pl.when(goal(k) >= 0)
            def _():
                fetch(k).start()
            return carry

        lax.fori_loop(0, slots, begin, 0)
        for owned in range(cl_own):
            count = place[0, OWN_CAP + owned]
            end = place[0, OWN_CAP + cl_own + owned] + count

            @pl.when(lax.rem(count, 2) == 1)
            def _():
                sorted_blocks[pl.ds(pl.multiple_of(end * blk, blk), blk), :] = jnp.zeros(
                    (blk, sorted_blocks.shape[1]), sorted_blocks.dtype
                )

        def finish(k, carry):
            @pl.when(goal(k) >= 0)
            def _():
                fetch(k).wait()
            return carry

        lax.fori_loop(0, slots, finish, 0)

    count = place[0, OWN_CAP + group]
    base = place[0, OWN_CAP + cl_own + group]
    steps = lax.div(count + 1, 2)

    def rows_of(step):
        return pl.ds(pl.multiple_of((base + 2 * step) * blk, blk), step_rows)

    @pl.when(part == 0)
    def _():
        def score(step, carry):
            rows = sorted_blocks[rows_of(step), :]
            wide = rows.astype(jnp.float32)
            weight = lax.rsqrt(jnp.mean(wide * wide, axis=1, keepdims=True) + 1e-06)
            raw = lax.dot_general(rows, train[0], (((1,), (1,)), ((), ())), preferred_element_type=jnp.float32)
            scores[pl.ds(pl.multiple_of(step * step_rows, step_rows), step_rows), :] = (raw * weight).astype(scores.dtype)
            return carry

        lax.fori_loop(0, steps, score, 0)

    columns = pl.ds(pl.multiple_of(part * tile, tile), tile)

    def terms(step, some):
        rows = pl.ds(pl.multiple_of((base + 2 * step) * blk, blk), some)
        left = sorted_blocks[rows, columns]
        contract = (((0,), (0,)), ((), ()))
        a = lax.dot_general(left, sorted_blocks[rows, :], contract, preferred_element_type=jnp.float32)
        part_scores = scores[pl.ds(pl.multiple_of(step * step_rows, step_rows), some), :]
        b = lax.dot_general(left, part_scores, contract, preferred_element_type=jnp.float32)
        return a * factor, b * factor

    odd = lax.rem(steps, 2)

    def first(some):
        a, b = terms(0, some)
        gram[0] = a
        cross[0] = b

    @pl.when(count == 0)
    def _():
        gram[...] = jnp.zeros_like(gram)
        cross[...] = jnp.zeros_like(cross)

    @pl.when(odd == 1)
    def _():
        first(step_rows)

    @pl.when((count > 0) & (odd == 0))
    def _():
        first(2 * step_rows)

    def add(pair, carry):
        a, b = terms(2 * pair + odd, 2 * step_rows)
        gram[0] += a
        cross[0] += b
        return carry

    lax.fori_loop(1 - odd, lax.div(steps, 2), add, 0)


def products(blocks, place, train):
    slots, blk, width = blocks.shape
    cl_own, mq, _ = train.shape
    tile = 256
    return pl.pallas_call(
        functools.partial(product_kernel, slots, cl_own, blk, tile, 1.0 / MEANROWS),
        out_shape=(
            jax.ShapeDtypeStruct((cl_own, width, width), jnp.float32),
            jax.ShapeDtypeStruct((cl_own, width, mq), jnp.float32),
        ),
        grid_spec=pltpu.PrefetchScalarGridSpec(
            num_scalar_prefetch=1,
            grid=(cl_own, width // tile),
            in_specs=[
                pl.BlockSpec(memory_space=pl.ANY),
                pl.BlockSpec((1, mq, width), lambda g, i, place: (g, 0, 0)),
            ],
            out_specs=(
                pl.BlockSpec((1, tile, width), lambda g, i, place: (g, i, 0)),
                pl.BlockSpec((1, tile, mq), lambda g, i, place: (g, i, 0)),
            ),
            scratch_shapes=[
                pltpu.VMEM(((slots + cl_own) * blk, width), blocks.dtype),
                pltpu.VMEM(((slots + 2) * blk, mq), blocks.dtype),
                pltpu.SemaphoreType.DMA((slots,)),
            ],
        ),
        compiler_params=pltpu.CompilerParams(
            dimension_semantics=("arbitrary", "arbitrary"), vmem_limit_bytes=60 * 1024 * 1024
        ),
        name="products",
    )(place, blocks, train)


def local(points, block_cluster, queries, query_ids):
    own_blocks, place, train = route(
        points, block_cluster, queries, query_ids, lax.axis_size("dp"), lax.axis_size("clus")
    )
    return products(own_blocks, place, train)


def solution(mesh):
    placed = (
        P(("dp", "clus"), None, None),
        P(("dp", "clus"), None),
        P(("dp", "clus"), None),
        P(("dp", "clus"), None),
    )
    return jax.shard_map(
        local,
        mesh=mesh,
        in_specs=placed,
        out_specs=(P(("dp", "clus"), None, None), P(("dp", "clus"), None, None)),
        check_vma=False,
    )
```

```python
import functools

import jax
import jax.numpy as jnp
from jax import lax
from jax.experimental import pallas as pl
from jax.experimental.pallas import tpu as pltpu
from jax.sharding import PartitionSpec as P

MEANROWS = 256
MESH = pl.DeviceIdType.MESH
RING = 4
AHEAD = 3
MID_CAP = 8
OWN_CAP = 3
ROWS = 16
LANES = 128
FIRST_SPLIT = (8, 8, 4, 2)
OTHER_SPLIT = (4, 4, 4, 4)
LAST_SPLIT = (2, 4, 4)


def lanes_of(shape):
    return lax.broadcasted_iota(jnp.int32, shape, 1)


def shifted(values, amount):
    return jnp.where(lanes_of(values.shape) >= amount, pltpu.roll(values, amount, axis=1), 0)


def before(mask):
    total = mask
    step = 1
    while step < LANES:
        total = total + shifted(total, step)
        step *= 2
    return total - mask


def rows_sum(values):
    return jnp.broadcast_to(jnp.sum(values, axis=1, keepdims=True), values.shape)


def tall(values, rows):
    return jnp.broadcast_to(values[0:1, :], (rows, LANES))


def route_kernel(pieces, nb, blk, width, n_dp, n_clus, cl_own, mq, *refs):
    labels, pts, queries, ids = refs[:4]
    out, place, train = refs[4:7]
    scratch = refs[7:]
    steps = len(pieces)
    total = 2 * steps
    half = blk // 2
    got1, pack2, got2, pack3 = (scratch[i * total:(i + 1) * total] for i in range(4))
    (
        s1, r1, s2, r2, s3, r3, own,
        mine, got_x, got_y, ring_label, got_r, row_label, got_d,
        tab_a, tab_b, tab_c, tab_d, sm_a, sm_b, sm_c, sm_d,
        sx, rx, sy, ry, sr, rr, sd, rd, tsem,
        q_dp, q_a, q_b, q_a2, q_b2, sq0, rq0, sqa1, rqa1, sqb1, rqb1, sqa2, rqa2, sqb2, rqb2, sq3, rq3,
        picked,
    ) = scratch[4 * total:]
    dp = lax.axis_index("dp")
    cl = lax.axis_index("clus")
    y, x = lax.div(cl, RING), lax.rem(cl, RING)
    core = lax.rem(dp, 2)
    clus_bits = n_clus.bit_length() - 1
    own_bits = cl_own.bit_length() - 1

    def along_x(delta):
        at = lax.rem(x + delta, RING)
        return at, (dp, y * RING + at)

    def along_y(delta):
        at = lax.rem(y + delta, RING)
        return at, (dp, at * RING + x)

    def peer(cls, stage, delta):
        return along_x(delta) if (cls == 0) == (stage == 1) else along_y(delta)

    def row_peer(delta):
        at = lax.rem(dp + delta, n_dp)
        return at, (at, cl)

    def send(src, dst, send_sem, recv_sem, device):
        return pltpu.make_async_remote_copy(
            src_ref=src, dst_ref=dst, send_sem=send_sem, recv_sem=recv_sem, device_id=device, device_id_type=MESH
        )

    barrier = pltpu.get_barrier_semaphore()
    friends = [along_x(d)[1] for d in range(1, RING)] + [along_y(d)[1] for d in range(1, RING)]
    friends += [row_peer(d)[1] for d in range(1, n_dp)]
    for friend in friends:
        pl.semaphore_signal(barrier, inc=1, device_id=friend, device_id_type=MESH)

    lane8 = lanes_of((8, LANES))
    vector = jnp.zeros((8, LANES), jnp.int32)
    for j in range(nb):
        vector = jnp.where(lane8 == cl * nb + j, labels[0, j] + 1, vector)
    mine[...] = vector

    pl.semaphore_wait(barrier, len(friends))

    def spot(step, cls):
        row0, c0, wide = pieces[step]
        return pl.ds(row0 + cls * half, ROWS), pl.ds(c0, wide)

    def copies1(step, cls):
        q = 2 * step + cls
        rows, cols = spot(step, cls)
        me = x if cls == 0 else y
        return [
            send(pts.at[:, rows, cols], got1[q].at[pl.ds(me * nb, nb)], s1.at[q, d - 1], r1.at[q, d - 1], peer(cls, 1, d)[1])
            for d in (1, RING - 1)
        ]

    def relays1(step, cls):
        q = 2 * step + cls
        me = x if cls == 0 else y
        part = nb // 2
        made = []
        for k, d in enumerate((1, RING - 1)):
            at = pl.ds(lax.rem(me + RING - d, RING) * nb + k * part, part)
            made.append(
                send(got1[q].at[at], got1[q].at[at], s1.at[q, 1 + 2 * k], r1.at[q, 1 + 2 * k], peer(cls, 1, d)[1])
            )
        return made

    def copies2(step, cls):
        q = 2 * step + cls
        me = y if cls == 0 else x
        made = []
        for d in range(1, RING):
            at, device = peer(cls, 2, d)
            made.append(
                send(
                    pack2[q].at[pl.ds(at * MID_CAP, MID_CAP)],
                    got2[q].at[pl.ds(me * MID_CAP, MID_CAP)],
                    s2.at[q, d - 1], r2.at[q, d - 1], device,
                )
            )
        return made

    def copies3(step, cls):
        q = 2 * step + cls
        rows, cols = spot(step, cls)
        made = []
        for d in range(1, n_dp):
            at, device = row_peer(d)
            made.append(
                send(
                    pack3[q].at[pl.ds(at * OWN_CAP, OWN_CAP)],
                    out.at[pl.ds(dp * OWN_CAP, OWN_CAP), rows, cols],
                    s3.at[q, d - 1], r3.at[q, d - 1], device,
                )
            )
        return made

    def own_copy(step, cls):
        q = 2 * step + cls
        rows, cols = spot(step, cls)
        return pltpu.make_async_copy(
            pack3[q].at[pl.ds(dp * OWN_CAP, OWN_CAP)], out.at[pl.ds(dp * OWN_CAP, OWN_CAP), rows, cols], own.at[q]
        )

    def labels_x():
        return [send(mine, got_x.at[d - 1], sx.at[d - 1], rx.at[d - 1], along_x(d)[1]) for d in range(1, RING)]

    def labels_y():
        return [send(mine, got_y.at[d - 1], sy.at[d - 1], ry.at[d - 1], along_y(d)[1]) for d in range(1, RING)]

    def labels_r():
        return [send(ring_label, got_r.at[d - 1], sr.at[d - 1], rr.at[d - 1], along_y(d)[1]) for d in range(1, RING)]

    def labels_d():
        return [send(row_label, got_d.at[d - 1], sd.at[d - 1], rd.at[d - 1], row_peer(d)[1]) for d in range(1, n_dp)]

    part = width // 2
    quarter = part // 2

    def queries_dp():
        made = []
        for d in range(1, n_dp):
            at, device = row_peer(d)
            cols = pl.ds(pl.multiple_of(lax.rem(at, 2) * part, part), part)
            made.append(send(queries.at[:, cols], q_dp.at[dp], sq0.at[d - 1], rq0.at[d - 1], device))
        return made

    def queries_first():
        a = [
            send(q_dp.at[:, :, pl.ds(0, quarter)], q_a.at[y, x], sqa1.at[d - 1], rqa1.at[d - 1], along_x(d)[1])
            for d in range(1, RING)
        ]
        b = [
            send(q_dp.at[:, :, pl.ds(quarter, quarter)], q_b.at[y, x], sqb1.at[d - 1], rqb1.at[d - 1], along_y(d)[1])
            for d in range(1, RING)
        ]
        return a + b

    def queries_second():
        ends = (1, RING - 1)
        a = [send(q_a.at[y], q_a.at[y], sqa2.at[d - 1], rqa2.at[d - 1], along_y(d)[1]) for d in ends]
        b = [send(q_b.at[:, x], q_b.at[:, x], sqb2.at[d - 1], rqb2.at[d - 1], along_x(d)[1]) for d in ends]
        return a + b

    def queries_relay():
        part = RING // 2
        made = []
        for k, d in enumerate((1, RING - 1)):
            some = pl.ds(k * part, part)
            a = q_a.at[lax.rem(y + RING - d, RING), some]
            b = q_b.at[some, lax.rem(x + RING - d, RING)]
            made.append(send(a, a, sqa2.at[1 + 2 * k], rqa2.at[1 + 2 * k], along_y(d)[1]))
            made.append(send(b, b, sqb2.at[1 + 2 * k], rqb2.at[1 + 2 * k], along_x(d)[1]))
        return made

    def queries_swap():
        device = (dp + 1 - 2 * core, cl)
        return [
            send(q_a, q_a2, sq3.at[0], rq3.at[0], device),
            send(q_b, q_b2, sq3.at[1], rq3.at[1], device),
        ]

    def start(copies):
        for copy in copies:
            copy.start()

    def start1(step):
        for cls in (0, 1):
            start(copies1(step, cls))

    def relay1(step):
        for cls in (0, 1):
            for copy in copies1(step, cls):
                copy.wait_recv()
            start(relays1(step, cls))

    def own1(step):
        for cls in (0, 1):
            rows, cols = spot(step, cls)
            me = x if cls == 0 else y
            got1[2 * step + cls][pl.ds(me * nb, nb)] = pts[:, rows, cols]

    def columns_of(values):
        return jnp.right_shift(values - 1, own_bits) & (n_clus - 1)

    def to_scalars(at, first, first_out, second, second_out):
        copies = [
            pltpu.make_async_copy(first, first_out, tsem.at[at]),
            pltpu.make_async_copy(second, second_out, tsem.at[at + 1]),
        ]
        start(copies)
        for copy in copies:
            copy.wait()

    def tables12():
        for copy in labels_x():
            copy.wait_recv()
        ring_x = mine[...]
        for d in range(1, RING):
            ring_x = ring_x + got_x[d - 1]
        ring_label[...] = ring_x
        for copy in labels_y():
            copy.wait_recv()
        ring_y = mine[...]
        for d in range(1, RING):
            ring_y = ring_y + got_y[d - 1]
        relay1(0)
        start(labels_r())
        count = RING * MID_CAP
        lane = lanes_of((count, LANES))
        row = lax.broadcasted_iota(jnp.int32, (count, LANES), 0)
        peer_at, slot = jnp.right_shift(row, 3), row & (MID_CAP - 1)
        for tab, values, wanted, index in (
            (tab_a, ring_x, peer_at * RING + x, lane & (RING * nb - 1)),
            (tab_b, ring_y, y * RING + peer_at, jnp.right_shift(lane, 4) * nb + (lane & (nb - 1))),
        ):
            values = tall(values, count)
            hit = ((values > 0) & (columns_of(values) == wanted)).astype(jnp.int32)
            tab[...] = rows_sum(jnp.where((hit > 0) & (before(hit) == slot), index, 0))
        relay1(1)
        for step in range(AHEAD):
            own1(step)
        to_scalars(0, tab_a, sm_a, tab_b, sm_b)

    def tables3():
        for copy in labels_r():
            copy.wait_recv()
        row_v = ring_label[...]
        for d in range(1, RING):
            row_v = row_v + got_r[d - 1]
        row_label[...] = row_v
        hit = ((row_v > 0) & (columns_of(row_v) == cl)).astype(jnp.int32)
        lane = lane8
        inside = lane & (RING * nb - 1)
        count = hit
        step = 1
        while step < RING * nb:
            count = count + jnp.where(inside >= step, pltpu.roll(count, step, axis=1), 0)
            step *= 2
        at_a = jnp.right_shift(lane, 4) * MID_CAP + count - hit
        earlier = hit
        for step in (RING * nb, 2 * RING * nb):
            earlier = earlier + shifted(earlier, step)
        earlier = earlier - hit
        j = lane & (nb - 1)
        rank = earlier
        for step in range(1, nb):
            rank = rank + jnp.where(j >= step, pltpu.roll(earlier + hit, step, axis=1), 0)
            rank = rank + jnp.where(j < nb - step, pltpu.roll(earlier, LANES - step, axis=1), 0)
        at_b = (jnp.right_shift(lane, 2) & (RING - 1)) * MID_CAP + rank
        count = n_dp * OWN_CAP
        values = tall(row_v, count)
        row = lax.broadcasted_iota(jnp.int32, (count, LANES), 0)
        to_row, slot = row & (n_dp - 1), jnp.right_shift(row, 3)
        row_of = jnp.right_shift(values - 1, own_bits + clus_bits)
        hit = ((values > 0) & (columns_of(values) == cl) & (row_of == to_row)).astype(jnp.int32)
        chosen = (hit > 0) & (before(hit) == slot)
        tab_c[...] = rows_sum(jnp.where(chosen, tall(at_a, count), 0))
        tab_d[...] = rows_sum(jnp.where(chosen, tall(at_b, count), 0))
        start(labels_d())
        to_scalars(2, tab_c, sm_c, tab_d, sm_d)

    def place_slots():
        for copy in labels_d():
            copy.wait_recv()
        sub = lax.broadcasted_iota(jnp.int32, (n_dp, LANES), 0)
        everything = jnp.where(sub == dp, row_label[...], 0)
        for d in range(1, n_dp):
            everything = jnp.where(sub == lax.rem(dp + n_dp - d, n_dp), got_d[d - 1], everything)
        here = dp * n_clus + cl
        hit = ((everything > 0) & (jnp.right_shift(everything - 1, own_bits) == here)).astype(jnp.int32)
        rank = before(hit)
        local = ((everything - 1) & (cl_own - 1)) + 1
        kinds = [rows_sum(jnp.where((hit > 0) & (rank == k), local, 0)) for k in range(OWN_CAP)]
        positions = [jnp.full((n_dp, LANES), -1, jnp.int32) for _ in range(OWN_CAP)]
        base = jnp.zeros((n_dp, LANES), jnp.int32)
        result = jnp.zeros((n_dp, LANES), jnp.int32)
        lane = lanes_of((n_dp, LANES))
        for owned in range(cl_own):
            marks = [(kind == owned + 1).astype(jnp.int32) for kind in kinds]
            per_row = sum(marks[1:], marks[0])
            running = per_row
            step = 1
            while step < n_dp:
                running = running + jnp.where(sub >= step, pltpu.roll(running, step, axis=0), 0)
                step *= 2
            ahead = base + running - per_row
            for k in range(OWN_CAP):
                positions[k] = jnp.where(marks[k] > 0, ahead, positions[k])
                ahead = ahead + marks[k]
            count = jnp.broadcast_to(jnp.sum(per_row, axis=0, keepdims=True), (n_dp, LANES))
            result = jnp.where(lane == OWN_CAP + owned, count, result)
            result = jnp.where(lane == OWN_CAP + cl_own + owned, base, result)
            base = base + jnp.right_shift(count + 1, 1) * 2
        for k in range(OWN_CAP):
            result = jnp.where(lane == k, positions[k], result)
        place[...] = result

    def step12(step):
        for cls in (0, 1):
            q = 2 * step + cls
            mid = y if cls == 0 else x
            for copy in relays1(step, cls):
                copy.wait_recv()
            sm = (sm_a, sm_b)[cls]

            def pack(k, carry, q=q, sm=sm):
                pack2[q][k] = got1[q][sm[k, 0]]
                return carry

            lax.fori_loop(0, RING * MID_CAP, pack, 0, unroll=8)
            start(copies2(step, cls))
            got2[q][pl.ds(mid * MID_CAP, MID_CAP)] = pack2[q][pl.ds(mid * MID_CAP, MID_CAP)]

    def step23(step):
        for cls in (0, 1):
            q = 2 * step + cls
            for copy in copies2(step, cls):
                copy.wait_recv()
            sm = (sm_c, sm_d)[cls]

            def pack(d, carry, q=q, sm=sm):
                for k in range(OWN_CAP):
                    pack3[q][d * OWN_CAP + k] = got2[q][sm[k * n_dp + d, 0]]
                return carry

            lax.fori_loop(0, n_dp, pack, 0, unroll=4)
            start(copies3(step, cls))
            own_copy(step, cls).start()

    def pick_train():
        group = RING * n_dp * queries.shape[0]
        per = queries.shape[0]
        per_bits = per.bit_length() - 1
        row = lax.broadcasted_iota(jnp.int32, (group, mq), 0)
        inner = row & (n_dp * per - 1)
        at_x = jnp.right_shift(row, per_bits + 3)
        stripe = jnp.right_shift(inner, per_bits) * (n_clus * per) + at_x * per + (inner & (per - 1))
        for owned in range(cl_own):
            wanted = jnp.clip(ids[owned:owned + 1, :], 0, n_dp * n_clus * per - 1)

            def add(at_y, carry, owned=owned, wanted=wanted):
                chosen = jnp.where(stripe + at_y * (RING * per) == wanted, 1.0, 0.0).astype(queries.dtype)
                for source, side, which in ((q_a, 0, 0), (q_b, 0, 1), (q_a2, 1, 0), (q_b2, 1, 1)):
                    values = source[at_y].reshape(group, quarter)
                    term = lax.dot_general(
                        chosen, values, (((0,), (0,)), ((), ())), preferred_element_type=jnp.float32
                    )
                    picked[owned, 2 * side + which] += term
                return carry

            lax.fori_loop(0, RING, add, 0)

    start(labels_x())
    start(labels_y())
    start(queries_dp())
    for step in range(AHEAD):
        start1(step)
    q_dp[dp] = queries[:, pl.ds(pl.multiple_of(core * part, part), part)]
    picked[...] = jnp.zeros_like(picked)
    tables12()
    for step in range(steps + 1):
        if step < steps:
            step12(step)
        if step >= 1:
            step23(step - 1)
        if step + 2 < steps:
            relay1(step + 2)
        if step + AHEAD < steps:
            start1(step + AHEAD)
            own1(step + AHEAD)
        if step == 0:
            tables3()
        if step == 1:
            for copy in queries_dp():
                copy.wait_recv()
            q_a[y, x] = q_dp[:, :, pl.ds(0, quarter)]
            q_b[y, x] = q_dp[:, :, pl.ds(quarter, quarter)]
            start(queries_first())
        if step == steps - 5:
            for copy in queries_first():
                copy.wait_recv()
            start(queries_second())
        if step == steps - 4:
            for copy in queries_second():
                copy.wait_recv()
            start(queries_relay())
        if step == steps - 3:
            place_slots()
        if step == steps - 2:
            for copy in queries_relay():
                copy.wait_recv()
            start(queries_swap())
    for copy in queries_swap():
        copy.wait_recv()
    pick_train()
    for owned in range(cl_own):
        for which in range(2):
            for side in range(2):
                at = lax.rem(core + side, 2) * part + which * quarter
                train[owned, :, pl.ds(pl.multiple_of(at, quarter), quarter)] = picked[owned, 2 * side + which].astype(
                    train.dtype
                )
    finished = labels_x() + labels_y() + labels_r() + labels_d()
    finished += queries_dp() + queries_first() + queries_second() + queries_relay() + queries_swap()
    for step in range(steps):
        for cls in (0, 1):
            finished += copies1(step, cls) + relays1(step, cls) + copies2(step, cls)
    for copy in finished:
        copy.wait_send()
    for step in range(steps):
        for cls in (0, 1):
            for copy in copies3(step, cls):
                copy.wait()
            own_copy(step, cls).wait()


def route(points, block_cluster, queries, query_ids, n_dp, n_clus):
    nb, blk, width = points.shape
    cl_own, mq = query_ids.shape
    per = queries.shape[0]
    kind = points.dtype
    pieces = []
    for row0 in range(0, blk // 2, ROWS):
        at = 0
        last = row0 + ROWS == blk // 2
        for part in FIRST_SPLIT if row0 == 0 else LAST_SPLIT if last else OTHER_SPLIT:
            wide = width // part
            pieces.append((row0, at, wide))
            at += wide
    total = 2 * len(pieces)
    dma = pltpu.SemaphoreType.DMA

    def many(count):
        return [pltpu.VMEM((count, ROWS, wide), kind) for _, _, wide in pieces for _ in range(2)]

    def pair(*shape):
        return [dma(shape), dma(shape)]

    def ints(*shape):
        return pltpu.VMEM(shape + (LANES,), jnp.int32)

    mid_rows, own_rows = RING * MID_CAP, n_dp * OWN_CAP
    scratch = many(RING * nb) + many(RING * MID_CAP) * 2 + many(n_dp * OWN_CAP)
    scratch += pair(total, RING) + pair(total, RING - 1) + pair(total, n_dp - 1) + [dma((total,))]
    scratch += [ints(8), ints(RING - 1, 8), ints(RING - 1, 8), ints(8), ints(RING - 1, 8), ints(8), ints(n_dp - 1, 8)]
    scratch += [ints(mid_rows), ints(mid_rows), ints(own_rows), ints(own_rows)]
    scratch += [pltpu.SMEM((rows, LANES), jnp.int32) for rows in (mid_rows, mid_rows, own_rows, own_rows)]
    scratch += pair(RING - 1) * 3 + pair(n_dp - 1) + [dma((4,))]
    quarter = width // 4
    scratch += [pltpu.VMEM((n_dp, per, width // 2), kind)]
    scratch += [pltpu.VMEM((RING, RING, n_dp, per, quarter), kind)] * 4
    scratch += pair(n_dp - 1) + pair(RING - 1) * 2 + pair(RING) * 2 + pair(2)
    scratch += [pltpu.VMEM((cl_own, 4, mq, quarter), jnp.float32)]
    vmem = pl.BlockSpec(memory_space=pltpu.VMEM)
    return pl.pallas_call(
        functools.partial(route_kernel, pieces, nb, blk, width, n_dp, n_clus, cl_own, mq),
        out_shape=(
            jax.ShapeDtypeStruct((n_dp * OWN_CAP, blk, width), kind),
            jax.ShapeDtypeStruct((n_dp, LANES), jnp.int32),
            jax.ShapeDtypeStruct((cl_own, mq, width), kind),
        ),
        in_specs=[pl.BlockSpec(memory_space=pltpu.SMEM), vmem, vmem, vmem],
        out_specs=(pl.BlockSpec(memory_space=pl.ANY), vmem, vmem),
        scratch_shapes=scratch,
        compiler_params=pltpu.CompilerParams(
            collective_id=0, has_side_effects=True, vmem_limit_bytes=60 * 1024 * 1024
        ),
        name="route",
    )(block_cluster.reshape(1, nb), points, queries, query_ids)


def product_kernel(slots, cl_own, blk, tile, factor, place, blocks, train, gram, cross, sorted_blocks, scores, sem):
    group = pl.program_id(0)
    part = pl.program_id(1)
    step_rows = 2 * blk

    def goal(k):
        return place[lax.div(k, OWN_CAP), lax.rem(k, OWN_CAP)]

    def fetch(k):
        rows = pl.ds(pl.multiple_of(goal(k) * blk, blk), blk)
        return pltpu.make_async_copy(blocks.at[k], sorted_blocks.at[rows], sem.at[k])

    @pl.when((group == 0) & (part == 0))
    def _():
        def begin(k, carry):
            @pl.when(goal(k) >= 0)
            def _():
                fetch(k).start()
            return carry

        lax.fori_loop(0, slots, begin, 0)
        for owned in range(cl_own):
            count = place[0, OWN_CAP + owned]
            end = place[0, OWN_CAP + cl_own + owned] + count

            @pl.when(lax.rem(count, 2) == 1)
            def _():
                sorted_blocks[pl.ds(pl.multiple_of(end * blk, blk), blk), :] = jnp.zeros(
                    (blk, sorted_blocks.shape[1]), sorted_blocks.dtype
                )

        def finish(k, carry):
            @pl.when(goal(k) >= 0)
            def _():
                fetch(k).wait()
            return carry

        lax.fori_loop(0, slots, finish, 0)

    count = place[0, OWN_CAP + group]
    base = place[0, OWN_CAP + cl_own + group]
    steps = lax.div(count + 1, 2)

    def rows_of(step):
        return pl.ds(pl.multiple_of((base + 2 * step) * blk, blk), step_rows)

    @pl.when(part == 0)
    def _():
        def score(step, carry):
            rows = sorted_blocks[rows_of(step), :]
            wide = rows.astype(jnp.float32)
            weight = lax.rsqrt(jnp.mean(wide * wide, axis=1, keepdims=True) + 1e-06)
            raw = lax.dot_general(rows, train[0], (((1,), (1,)), ((), ())), preferred_element_type=jnp.float32)
            scores[pl.ds(pl.multiple_of(step * step_rows, step_rows), step_rows), :] = (raw * weight).astype(scores.dtype)
            return carry

        lax.fori_loop(0, steps, score, 0)

    columns = pl.ds(pl.multiple_of(part * tile, tile), tile)

    def terms(step, some):
        rows = pl.ds(pl.multiple_of((base + 2 * step) * blk, blk), some)
        left = sorted_blocks[rows, columns]
        contract = (((0,), (0,)), ((), ()))
        a = lax.dot_general(left, sorted_blocks[rows, :], contract, preferred_element_type=jnp.float32)
        part_scores = scores[pl.ds(pl.multiple_of(step * step_rows, step_rows), some), :]
        b = lax.dot_general(left, part_scores, contract, preferred_element_type=jnp.float32)
        return a * factor, b * factor

    odd = lax.rem(steps, 2)

    def first(some):
        a, b = terms(0, some)
        gram[0] = a
        cross[0] = b

    @pl.when(count == 0)
    def _():
        gram[...] = jnp.zeros_like(gram)
        cross[...] = jnp.zeros_like(cross)

    @pl.when(odd == 1)
    def _():
        first(step_rows)

    @pl.when((count > 0) & (odd == 0))
    def _():
        first(2 * step_rows)

    def add(pair, carry):
        a, b = terms(2 * pair + odd, 2 * step_rows)
        gram[0] += a
        cross[0] += b
        return carry

    lax.fori_loop(1 - odd, lax.div(steps, 2), add, 0)


def products(blocks, place, train):
    slots, blk, width = blocks.shape
    cl_own, mq, _ = train.shape
    tile = 256
    return pl.pallas_call(
        functools.partial(product_kernel, slots, cl_own, blk, tile, 1.0 / MEANROWS),
        out_shape=(
            jax.ShapeDtypeStruct((cl_own, width, width), jnp.float32),
            jax.ShapeDtypeStruct((cl_own, width, mq), jnp.float32),
        ),
        grid_spec=pltpu.PrefetchScalarGridSpec(
            num_scalar_prefetch=1,
            grid=(cl_own, width // tile),
            in_specs=[
                pl.BlockSpec(memory_space=pl.ANY),
                pl.BlockSpec((1, mq, width), lambda g, i, place: (g, 0, 0)),
            ],
            out_specs=(
                pl.BlockSpec((1, tile, width), lambda g, i, place: (g, i, 0)),
                pl.BlockSpec((1, tile, mq), lambda g, i, place: (g, i, 0)),
            ),
            scratch_shapes=[
                pltpu.VMEM(((slots + cl_own) * blk, width), blocks.dtype),
                pltpu.VMEM(((slots + 2) * blk, mq), blocks.dtype),
                pltpu.SemaphoreType.DMA((slots,)),
            ],
        ),
        compiler_params=pltpu.CompilerParams(
            dimension_semantics=("arbitrary", "arbitrary"), vmem_limit_bytes=60 * 1024 * 1024
        ),
        name="products",
    )(place, blocks, train)


def local(points, block_cluster, queries, query_ids):
    own_blocks, place, train = route(
        points, block_cluster, queries, query_ids, lax.axis_size("dp"), lax.axis_size("clus")
    )
    return products(own_blocks, place, train)


def solution(mesh):
    placed = (
        P(("dp", "clus"), None, None),
        P(("dp", "clus"), None),
        P(("dp", "clus"), None),
        P(("dp", "clus"), None),
    )
    return jax.shard_map(
        local,
        mesh=mesh,
        in_specs=placed,
        out_specs=(P(("dp", "clus"), None, None), P(("dp", "clus"), None, None)),
        check_vma=False,
    )
```
